128 devices in a mesh: row: 4 (over y), col: 32 (over z, x, core).
Axes of the slice: x: 4, y: 4, z: 4, core: 2. Of those that a mesh axis runs over, the one named last changes fastest.
Arguments:
- dofs: float32 [504, 32768], P(None, ('row', 'col')), may hold values from -6 to 6
- star: float32 [243, 32768], P(None, ('row', 'col')), may hold values from -1.25 to 1.25
- flux_mats: float32 [648, 32768], P(None, ('row', 'col')), may hold values from -0.75 to 0.75
- kxi: float32 [3, 56, 56], replicated, may hold values from -0.75 to 0.75
- face_proj: float32 [4, 56, 21], replicated, may hold values from -0.75 to 0.75
- face_lift: float32 [4, 21, 56], replicated, may hold values from -1.25 to 1.25
- orient: float32 [3, 21, 21], replicated, may hold values from -1.25 to 1.25
- neighbour: int32 [4, 32768], P(None, ('row', 'col')), may hold values from 0 to 2047
- orient_code: int32 [4, 32768], P(None, ('row', 'col')), may hold values from 0 to 2
- send_list: int32 [4, 8192], P(None, ('row', 'col')), may hold values from 0 to 255
- fault_part: int32 [16384, 1], P(('row', 'col')), may hold values from 0 to 127; in each aligned block of 128 rows (0 to 127, 128 to 255, ...) at most 2 rows name the same one
- fault_item: int32 [16384], P(('row', 'col')), may hold values from 0 to 1023
- shear_init: float32 [21, 16384], P(None, ('row', 'col')), may hold values from -8 to 8
- normal_init: float32 [21, 16384], P(None, ('row', 'col')), may hold values from 1 to 8
- state_var: float32 [21, 16384], P(None, ('row', 'col')), may hold values from 0.3 to 0.7
- slip_prev: float32 [21, 16384], P(None, ('row', 'col')), may hold values from 0.05 to 2
Outputs:
- dofs_next: float32 [504, 32768], P(None, ('row', 'col'))
- slip_rate: float32 [21, 16384], P(None, ('row', 'col'))
The draws below stay inside these ranges and needn't reach their ends.
Inputs may be any that keep to these rules, and one draw needn't show every extreme that they name: `fault_part`: partitions are numbered r * 32 + c. Among the 128 fault rows held by one device, no partition is named by more than 2 rows.
All inputs are finite; a program needn't handle non-finite values.
Results may differ from the reference program's by a relative error of at most 0.0003.
Values sent between devices are 32-bit elements; how exact they have to be, the bound alone decides.
A program may use at most 128 MiB of HBM per device.

```python
import math
import jax
import jax.numpy as jnp
import numpy as np
from jax import lax

QUANT = 9
BASIS = 56
FACE_BASIS = 21
ORDER = 6
NEWTON_ITERS = 3
ELEM_DEV = 256
FAULT_DEV = 128
GHOSTS = 64
MOST = 2
ELEMENTS = 32768
SENDS = 8192
FAULTS = 16384
N_ROW = 4
N_COL = 32


def plant(values, own_key, low, high):
    longest = values.shape.index(max(values.shape))
    spots = []
    for shift in (0, 1):
        where = [jax.random.randint(jax.random.fold_in(own_key, axis), (), 0, length) for axis, length in enumerate(values.shape)]
        where[longest] = (where[longest] + shift) % values.shape[longest]
        spots.append(tuple(where))
    return values.at[spots[0]].set(low).at[spots[1]].set(high)


def shard_levels(own_key, shape, shards, smallest, high):
    def one(axis_at, parts):
        steps = jax.random.uniform(jax.random.fold_in(jax.random.fold_in(own_key, 6), axis_at), (parts,), jnp.float32, smallest / len(shards), high / len(shards))
        return jnp.repeat(jnp.exp(steps), shape[axis_at] // parts).reshape((-1,) + (1,) * (len(shape) - axis_at - 1))

    factor_of = one(*shards[0])
    for cut in shards[1:]:
        factor_of = factor_of * one(*cut)
    return factor_of


def routed_block(rng, own, number, rows, amount, top, reach, slope):
    order = jax.random.permutation(rng, amount)
    heavy_load, ordinary = shares(amount, rows * top, reach, slope, True), shares(amount, rows * top, reach, slope, False)
    places = jnp.arange(amount)

    def named(lengths, rotation):
        used = int((lengths > 0).sum())
        fixed = max(1, used // 4)
        moved = fixed + (places - fixed + rotation * (used - fixed)) % max(1, amount - fixed)
        return jnp.zeros((amount,), jnp.int32).at[order[jnp.where(places < fixed, places, moved)]].set(jnp.asarray(lengths, jnp.int32))

    lengths = jnp.where(number % 4 == 0, named(heavy_load, number // 4), named(ordinary, number - number // 4 - 1))
    mixed = jax.random.permutation(jax.random.fold_in(own, 3), amount)
    giver, sink = mixed[0:amount // 2 * 2:2], mixed[1:amount // 2 * 2:2]
    margin = jnp.minimum(lengths[giver] - 1, reach - lengths[sink]) // 2
    margin = jnp.where((giver == order[0]) | (sink == order[0]) | (lengths[sink] == 0), 0, jnp.maximum(margin, 0))
    moved = jax.random.randint(jax.random.fold_in(own, 4), (amount // 2,), 0, 1 << 20) % (margin + 1)
    lengths = lengths.at[giver].add(-moved).at[sink].add(moved)
    items = jnp.searchsorted(jnp.cumsum(lengths), jnp.arange(rows * top), side="right").astype(jnp.int32)
    grid = items.reshape(top, rows).T
    grid = grid[jax.random.permutation(jax.random.fold_in(own, 1), rows)]
    rotation = jax.random.randint(jax.random.fold_in(own, 2), (rows, 1), 0, top)
    return jnp.take_along_axis(grid, (jnp.arange(top)[None, :] + rotation) % top, axis=1)


def shares(count, total, limit, skew, full):
    portions = [(1 << 20) // math.isqrt(grade ** skew) + 1 for grade in range(1, count + 1)]
    largest = limit if full else min(limit, max(-(-total // count), total * portions[0] // sum(portions)))
    least = 1 if total - largest >= count - 1 else 0
    holding, surplus = [largest] + [least] * (count - 1), total - largest - least * (count - 1)
    while surplus > 0:
        movable = [i for i in range(1, count) if holding[i] < largest] or [i for i in range(1, count) if holding[i] < limit]
        whole, remaining = sum([portions[i] for i in movable]), surplus
        for i in movable:
            addition = min(limit - holding[i], max(1, remaining * portions[i] // whole), surplus)
            holding[i] = holding[i] + addition
            surplus = surplus - addition
    return np.array(holding)


def scatter_about(rng, extent, scale, bound, cuts=(), kind=jnp.bfloat16):
    result = jax.random.normal(rng, extent, jnp.float32) * scale
    if len(cuts) > 0:
        result = shard_levels(rng, extent, cuts, -0.22, 0.18) * result
    return jnp.clip(result, min=-bound, max=bound).astype(kind)


def setup_inputs(seed: int = 0) -> dict:
    key_list = jax.random.split(jax.random.key(seed), 17)
    dofs = scatter_about(key_list[0], (QUANT * BASIS, ELEMENTS), 1.0, 6.0, ((1, 128),), jnp.float32)
    star = scatter_about(key_list[1], (3 * QUANT * QUANT, ELEMENTS), (3 * QUANT) ** -0.5, 1.25, ((1, 128),), jnp.float32)
    flux_mats = scatter_about(key_list[2], (8 * QUANT * QUANT, ELEMENTS), (8 * QUANT) ** -0.5, 0.75, ((1, 128),), jnp.float32)
    kxi = scatter_about(key_list[3], (3, BASIS, BASIS), BASIS ** -0.5, 0.75, (), jnp.float32)
    face_proj = scatter_about(key_list[4], (4, BASIS, FACE_BASIS), BASIS ** -0.5, 0.75, (), jnp.float32)
    face_lift = scatter_about(key_list[5], (4, FACE_BASIS, BASIS), FACE_BASIS ** -0.5, 1.25, (), jnp.float32)
    orient = scatter_about(key_list[6], (3, FACE_BASIS, FACE_BASIS), FACE_BASIS ** -0.5, 1.25, (), jnp.float32)
    neighbour = plant(jax.random.randint(key_list[7], (4, ELEMENTS), 0, 4 * ELEM_DEV + 16 * GHOSTS), jax.random.fold_in(key_list[7], 1), 0, (4 * ELEM_DEV + 16 * GHOSTS) - 1).astype(jnp.int32)
    orient_code = plant(jax.random.randint(key_list[8], (4, ELEMENTS), 0, 3), jax.random.fold_in(key_list[8], 1), 0, 2).astype(jnp.int32)
    send_list = plant(jax.random.randint(key_list[9], (4, SENDS), 0, ELEM_DEV), jax.random.fold_in(key_list[9], 1), 0, ELEM_DEV - 1).astype(jnp.int32)
    fault_part_keys = jax.random.split(jax.random.fold_in(key_list[10], 1), FAULTS // FAULT_DEV)
    fault_part_turns = jax.random.permutation(jax.random.fold_in(key_list[10], 3), FAULTS // FAULT_DEV)
    fault_part = jax.vmap(lambda own, number: routed_block(jax.random.fold_in(key_list[10], 2), own, number, FAULT_DEV, N_ROW * N_COL, 1, MOST, 2))(fault_part_keys, fault_part_turns).reshape((FAULTS, 1))
    fault_item = plant(jax.random.randint(key_list[11], (FAULTS,), 0, 4 * ELEM_DEV), jax.random.fold_in(key_list[11], 1), 0, (4 * ELEM_DEV) - 1).astype(jnp.int32)
    shear_init = scatter_about(key_list[12], (FACE_BASIS, FAULTS), 2.0, 8.0, ((1, 128),), jnp.float32)
    normal_init = jnp.clip(jnp.exp(math.log(8.0) - 2.0794415 * jax.random.uniform(key_list[13], (FACE_BASIS, FAULTS), jnp.float32) ** shard_levels(key_list[13], (FACE_BASIS, FAULTS), ((1, 128),), -0.2, 0.2)), 1.0, 8.0)
    state_var = jnp.clip(0.3 + 0.39999998 * jax.random.uniform(key_list[14], (FACE_BASIS, FAULTS), jnp.float32) ** shard_levels(key_list[14], (FACE_BASIS, FAULTS), ((1, 128),), -0.2, 0.2), 0.3, 0.7)
    slip_prev = jnp.clip(0.05 + 1.95 * jax.random.uniform(key_list[15], (FACE_BASIS, FAULTS), jnp.float32) ** shard_levels(key_list[15], (FACE_BASIS, FAULTS), ((1, 128),), -0.2, 0.2), 0.05, 2.0)
    return dict(dofs=dofs, star=star, flux_mats=flux_mats, kxi=kxi, face_proj=face_proj, face_lift=face_lift, orient=orient, neighbour=neighbour, orient_code=orient_code, send_list=send_list, fault_part=fault_part, fault_item=fault_item, shear_init=shear_init, normal_init=normal_init, state_var=state_var, slip_prev=slip_prev)


time_step = 2.0
fric_a = 0.5
highest = lax.Precision.HIGHEST

def inverse_sinh(value):
    magnitude = jnp.abs(value)
    squared = magnitude * magnitude
    positive = jnp.log1p(magnitude + squared / (1.0 + jnp.sqrt(1.0 + squared)))
    return jnp.where(value < 0.0, -positive, positive)

def small_apply(mats, values):
    total = mats[:, 0, None, :] * values[0][None, :, :]
    for inner in range(1, QUANT):
        total = total + mats[:, inner, None, :] * values[inner][None, :, :]
    return total

def face_apply(mats, values):
    total = jnp.transpose(mats[:, :, 0, :], (1, 0, 2))[:, None, :, :] * values[0][None, :, :, :]
    for inner in range(1, QUANT):
        total = total + jnp.transpose(mats[:, :, inner, :], (1, 0, 2))[:, None, :, :] * values[inner][None, :, :, :]
    return total

def predict(dofs_block, star_block, kxi):
    elem_count = dofs_block.shape[1]
    derivative = dofs_block.reshape(QUANT, BASIS, elem_count)
    star_mats = star_block.reshape(3, QUANT, QUANT, elem_count)
    factor = time_step
    integral = factor * derivative
    for order_k in range(1, ORDER):
        summed = jnp.zeros_like(derivative)
        for axis_dir in range(3):
            advected = jnp.einsum('qbe,bc->qce', derivative, kxi[axis_dir], precision=highest)
            summed = summed + small_apply(star_mats[axis_dir], advected)
        derivative = summed
        factor = factor * time_step / (order_k + 1)
        integral = integral + factor * derivative
    return integral

def volume_term(integral, star_block, kxi):
    elem_count = integral.shape[2]
    star_mats = star_block.reshape(3, QUANT, QUANT, elem_count)
    summed = jnp.zeros_like(integral)
    for axis_dir in range(3):
        turned = jnp.einsum('qbe,cb->qce', integral, kxi[axis_dir], precision=highest)
        summed = summed + small_apply(star_mats[axis_dir], turned)
    return summed

def surface_terms(traces, ghost_traces, flux_block, neighbour_b, code_b, face_lift, orient):
    elem_count = traces.shape[3]
    trace_table = jnp.concatenate([traces.reshape(QUANT, FACE_BASIS, 4 * elem_count), ghost_traces], axis=2)
    neighbour_vals = jnp.take(trace_table, neighbour_b.reshape(-1), axis=2).reshape(QUANT, FACE_BASIS, 4, elem_count)
    oriented = jnp.zeros_like(neighbour_vals)
    for turn in range(3):
        rotated = jnp.einsum('qgfe,gk->qkfe', neighbour_vals, orient[turn], precision=highest)
        oriented = jnp.where(code_b == turn, rotated, oriented)
    flux_view = flux_block.reshape(4, 2, QUANT, QUANT, elem_count)
    own_part = face_apply(flux_view[:, 0], traces)
    other_part = face_apply(flux_view[:, 1], oriented)
    flux_term = jnp.einsum('pgfe,fgb->pbe', own_part + other_part, face_lift, precision=highest)
    shear = 0.5 * (traces[3] + oriented[3]) + 0.5 * (traces[6] - oriented[6])
    normal = 0.5 * (traces[0] + oriented[0])
    fault_vals = jnp.stack([shear, normal]).reshape(2, FACE_BASIS, 4 * elem_count)
    return (flux_term, fault_vals)

def friction_solve(shear, normal, shear_init, normal_init, state_var, slip_prev):
    shear_total = shear_init + shear
    normal_eff = normal_init * (1.0 + 0.5 * jnp.tanh(normal))
    growth = jnp.exp(state_var / fric_a) * 0.5
    slip_now = slip_prev
    for newton_step in range(NEWTON_ITERS):
        scaled = growth * slip_now
        misfit = shear_total - slip_now - fric_a * normal_eff * inverse_sinh(scaled)
        slope_val = -1.0 - fric_a * normal_eff * growth / jnp.sqrt(1.0 + scaled * scaled)
        slip_now = slip_now - misfit / slope_val
    return slip_now

def reference(dofs, star, flux_mats, kxi, face_proj, face_lift, orient, neighbour, orient_code, send_list, fault_part, fault_item, shear_init, normal_init, state_var, slip_prev):
    devices = N_ROW * N_COL

    def blocks(array):
        return array.reshape(array.shape[0], devices, array.shape[1] // devices).transpose(1, 0, 2)
    integral_all = lax.map(lambda pair: predict(pair[0], pair[1], kxi), (blocks(dofs), blocks(star)))
    flat_all = integral_all.reshape(devices, QUANT * BASIS, ELEM_DEV)
    sent_rows = jax.vmap(lambda rows, picks: jnp.take(rows, picks, axis=1))(flat_all, blocks(send_list))
    by_grid = sent_rows.reshape(N_ROW, N_COL, QUANT * BASIS, 4, GHOSTS)
    empty_row = jnp.zeros((1, N_COL, QUANT * BASIS, GHOSTS), by_grid.dtype)
    empty_col = jnp.zeros((N_ROW, 1, QUANT * BASIS, GHOSTS), by_grid.dtype)
    from_lower_row = jnp.concatenate([empty_row, by_grid[:-1, :, :, 0]], axis=0)
    from_upper_row = jnp.concatenate([by_grid[1:, :, :, 1], empty_row], axis=0)
    from_lower_col = jnp.concatenate([empty_col, by_grid[:, :-1, :, 2]], axis=1)
    from_upper_col = jnp.concatenate([by_grid[:, 1:, :, 3], empty_col], axis=1)
    ghost_all = jnp.concatenate([from_lower_row, from_upper_row, from_lower_col, from_upper_col], axis=3)
    ghost_all = ghost_all.reshape(devices, QUANT, BASIS, 4 * GHOSTS)

    def local_step(pack):
        dofs_block, star_block, flux_block, neighbour_b, code_b, integral, ghost_elems = pack
        traces = jnp.einsum('qbe,jbf->qfje', integral, face_proj, precision=highest)
        ghost_traces = jnp.einsum('qbg,jbf->qfjg', ghost_elems, face_proj, precision=highest)
        ghost_traces = ghost_traces.reshape(QUANT, FACE_BASIS, 16 * GHOSTS)
        flux_term, fault_vals = surface_terms(traces, ghost_traces, flux_block, neighbour_b, code_b, face_lift, orient)
        updated = dofs_block.reshape(QUANT, BASIS, ELEM_DEV) + 0.25 * (volume_term(integral, star_block, kxi) + flux_term)
        return (updated, fault_vals)
    updated_all, fault_all = lax.map(local_step, (blocks(dofs), blocks(star), blocks(flux_mats), blocks(neighbour), blocks(orient_code), integral_all, ghost_all))
    host_part = fault_part[:, 0]
    face_of = fault_item // ELEM_DEV
    elem_of = fault_item % ELEM_DEV
    fault_table = fault_all.transpose(1, 2, 0, 3).reshape(2, FACE_BASIS, devices * 4 * ELEM_DEV)
    own_vals = jnp.take(fault_table, host_part * (4 * ELEM_DEV) + fault_item, axis=2)
    slip_rate = friction_solve(own_vals[0], own_vals[1], shear_init, normal_init, state_var, slip_prev)
    lifted_all = jnp.einsum('gs,jgb->jbs', slip_rate, face_lift, precision=highest)
    lifted = jnp.zeros_like(lifted_all[0])
    for face_idx in range(4):
        lifted = jnp.where(face_of[None, :] == face_idx, lifted_all[face_idx], lifted)
    fault_push = jnp.zeros((BASIS, ELEMENTS), lifted.dtype).at[:, host_part * ELEM_DEV + elem_of].add(lifted)
    updated = updated_all.transpose(1, 2, 0, 3).reshape(QUANT, BASIS, ELEMENTS)
    updated = updated.at[3].add(-0.5 * fault_push).at[6].add(0.5 * fault_push)
    return (updated.reshape(QUANT * BASIS, ELEMENTS), slip_rate)
```

```python
import jax
import jax.numpy as jnp
from jax import lax
from jax.experimental import pallas as pl
from jax.experimental.pallas import tpu as pltpu
from jax.sharding import PartitionSpec as P

QUANT = 9
BASIS = 56
FACE = 21
ORDER = 6
NEWTON_ITERS = 3
TIME_STEP = 2.0
FRIC_A = 0.5
MESH = pl.DeviceIdType.MESH
BF = jnp.bfloat16
F32 = jnp.float32

Q_ORDER = (0, 3, 6, 1, 2, 4, 5, 7, 8)
HEAD = 3 * 128


def iota(shape, dim):
    return lax.broadcasted_iota(jnp.int32, shape, dim)


def ones_at(mask):
    return jnp.where(mask, 1.0, 0.0).astype(BF)


def nn(a, b):
    return jnp.dot(a, b, preferred_element_type=F32)


def nt(a, b):
    return lax.dot_general(a, b, (((1,), (1,)), ((), ())), preferred_element_type=F32)


def split(x):
    high = x.astype(BF)
    return high, (x - high.astype(F32)).astype(BF)


def eye(rows, cols):
    return ones_at(iota((rows, cols), 0) == iota((rows, cols), 1))


def place(rows, cols, offsets):
    delta = iota((rows, cols), 1) - iota((rows, cols), 0)
    mask = delta == offsets[0]
    for offset in offsets[1:]:
        mask = mask | (delta == offset)
    return ones_at(mask)


def padded(x):
    return jnp.concatenate([x, jnp.zeros((8, x.shape[1]), F32)], axis=0)


def stacked(x):
    high, low = split(x)
    return jnp.concatenate([high, high, low], axis=0)


def inverse_sinh(value):
    magnitude = jnp.abs(value)
    squared = magnitude * magnitude
    positive = jnp.log1p(magnitude + squared / (1.0 + jnp.sqrt(1.0 + squared)))
    return jnp.where(value < 0.0, -positive, positive)


def friction_solve(shear, normal, shear_init, normal_init, state_var, slip_prev):
    shear_total = shear_init + shear
    normal_eff = normal_init * (1.0 + 0.5 * jnp.tanh(normal))
    growth = jnp.exp(state_var / FRIC_A) * 0.5
    slip_now = slip_prev
    for _ in range(NEWTON_ITERS):
        scaled = growth * slip_now
        misfit = shear_total - slip_now - FRIC_A * normal_eff * inverse_sinh(scaled)
        slope_val = -1.0 - FRIC_A * normal_eff * growth / jnp.sqrt(1.0 + scaled * scaled)
        slip_now = slip_now - misfit / slope_val
    return slip_now


def kernel(
    n_row, n_col,
    dofs, star, flux, kxi, proj, lift, orient, nbr, ocode, slist, fpart, fitem, sh0, nm0, stv, slp,
    out, slip_out,
    wk, wv, wp, wo, wl, adv, integ, ihl, xs, glb, gtab, nvals, comb, fvals, ohk, mpart,
    gsend, grecv, qsend, qrecv, asend, arecv, vsend, vrecv,
    gs_sem, gr_sem, q_sem, a_sem, v_sem, loc_sem,
):
    devices = n_row * n_col
    row, col = lax.axis_index("row"), lax.axis_index("col")
    me = row * n_col + col

    barrier = pltpu.get_barrier_semaphore()

    def partner(s):
        p = lax.rem(me + s, devices)
        return p, (p // n_col, lax.rem(p, n_col))

    def greet(s, _):
        _, where = partner(s)
        pl.semaphore_signal(barrier, inc=1, device_id=where, device_id_type=MESH)
        return 0

    lax.fori_loop(1, devices, greet, 0)

    def exchange_start(send, recv, sem, local_sem):
        def one(s, _):
            p, where = partner(s)
            pltpu.make_async_remote_copy(
                src_ref=send.at[pl.ds(p, 1)],
                dst_ref=recv.at[pl.ds(me, 1)],
                send_sem=sem.at[0],
                recv_sem=sem.at[1],
                device_id=where,
                device_id_type=MESH,
            ).start()
            return 0

        lax.fori_loop(1, devices, one, 0)
        pltpu.make_async_copy(send.at[pl.ds(me, 1)], recv.at[pl.ds(me, 1)], local_sem).start()

    def exchange_wait(send, recv, sem, local_sem):
        part = pl.ds(0, devices - 1)
        pltpu.make_async_copy(recv.at[part], recv.at[part], sem.at[1]).wait()
        pltpu.make_async_copy(send.at[pl.ds(me, 1)], recv.at[pl.ds(me, 1)], local_sem).wait()

    def exchange_end(send, sem):
        part = pl.ds(0, devices - 1)
        pltpu.make_async_copy(send.at[part], send.at[part], sem.at[0]).wait()

    at_high, at_low = place(BASIS, 192, (0, 128)), place(BASIS, 192, (64,))
    eye_b = eye(BASIS, BASIS)
    back, forth = [], []
    for d in range(3):
        high, low = split(kxi[d])
        forth.append(nn(high, at_high) + nn(low, at_low))
        back.append(nn(nt(eye_b, high).astype(BF), at_high) + nn(nt(eye_b, low).astype(BF), at_low))
    wk[...] = jnp.concatenate(back, axis=0).astype(BF)
    wv[...] = jnp.concatenate(forth, axis=0).astype(BF)
    rows = []
    pick_f = eye(32, FACE)
    for j in range(4):
        high, low = split(proj[j])
        rows.append(nn(nt(pick_f, high).astype(BF), at_high) + nn(nt(pick_f, low).astype(BF), at_low))
    wp[...] = jnp.concatenate(rows, axis=0).astype(BF)
    rows = []
    pick_g = eye(24, FACE)
    turn_high, turn_low = place(FACE, 96, (0, 64)), place(FACE, 96, (32,))
    for o in range(3):
        high, low = split(orient[o])
        rows.append(nn(nt(pick_g, high).astype(BF), turn_high) + nn(nt(pick_g, low).astype(BF), turn_low))
    wo[...] = jnp.concatenate(rows, axis=0).astype(BF)
    table = jnp.zeros((BASIS, 192), F32)
    for j in range(4):
        high, low = split(lift[j])
        table = table + nn(nt(eye_b, high).astype(BF), place(FACE, 192, (24 * j,)))
        table = table + nn(nt(eye_b, low).astype(BF), place(FACE, 192, (96 + 24 * j,)))
    wl[...] = table.astype(BF)

    square = (devices, fitem.shape[1])
    wide_part = jnp.broadcast_to(fpart[...], square)
    part_row = jnp.sum(jnp.where(iota(square, 0) == iota(square, 1), wide_part, 0), axis=0, keepdims=True)
    earlier = (wide_part == part_row) & (iota(square, 0) < iota(square, 1))
    rank_row = jnp.sum(jnp.where(earlier, 1, 0), axis=0, keepdims=True)
    names = iota(square, 0) == part_row
    mpart[0] = ones_at(names & (rank_row == 0))
    mpart[1] = ones_at(names & (rank_row == 1))
    code_row = (fitem[...] + 1).astype(F32)
    asked = [
        jnp.sum(jnp.where(names & (rank_row == k), code_row, 0.0), axis=1, keepdims=True) for k in range(2)
    ]
    low_lane = iota((devices, 128), 1) < 64
    qsend[...] = jnp.where(low_lane, asked[0], asked[1])

    def put(weights, value, target, q):
        target[q] = nn(weights[...], stacked(padded(value)))

    for q in range(QUANT):
        start = dofs[q * BASIS:(q + 1) * BASIS, :]
        integ[q] = TIME_STEP * start
        put(wk, start, adv.at[0], q)

    pl.semaphore_wait(barrier, devices - 1)
    exchange_start(qsend, qrecv, q_sem, loc_sem.at[0])

    def star_block(source, first):
        totals = [None] * 3
        for q in range(QUANT):
            for d in range(3):
                value = source[q, d * BASIS:(d + 1) * BASIS, :]
                for i in range(3):
                    r = (d * QUANT + first + i) * QUANT + q
                    term = star[r:r + 1, :] * value
                    totals[i] = term if totals[i] is None else totals[i] + term
        return totals

    factor = TIME_STEP
    for k in range(1, ORDER):
        factor = factor * TIME_STEP / (k + 1)
        source, target = adv.at[(k - 1) % 2], adv.at[k % 2]
        for first in range(0, QUANT, 3):
            for i, total in enumerate(star_block(source, first)):
                p = first + i
                if k < ORDER - 1:
                    integ[p] = integ[p] + factor * total
                    put(wk, total, target, p)
                else:
                    high, low = split(padded(integ[p] + factor * total))
                    block = Q_ORDER.index(p) * 128
                    ihl[block:block + 64, :] = high
                    ihl[block + 64:block + 128, :] = low
                    both = jnp.concatenate([high, high, low], axis=0)
                    target[p] = nn(wv[...], both)
                    xs[p] = nn(wp[...], both)
    turned = adv.at[(ORDER - 1) % 2]

    small = slist.shape[1]
    spread = ones_at(lax.rem(iota((small, 4 * small), 1), small) == iota((small, 4 * small), 0))
    listed = nn(slist[...].astype(F32).astype(BF), spread)
    listed = jnp.sum(
        jnp.where(iota((4, 4 * small), 1) // small == iota((4, 4 * small), 0), listed, 0.0), axis=0, keepdims=True
    ).astype(jnp.int32)
    elems = dofs.shape[1]
    picked = nn(ihl[...], ones_at(iota((elems, 4 * small), 0) == listed))
    half = iota((BASIS, 128), 1) < 64

    def pick(q, side):
        block = Q_ORDER.index(q) * 128
        lanes = slice(side * 128, side * 128 + 128)
        return picked[block:block + BASIS, lanes] + picked[block + 64:block + 64 + BASIS, lanes]

    for side in range(2):
        for q in range(5):
            first = pick(q, side)
            second = pick(q + 5, side) if q < 4 else first
            gsend[2 * side, q] = jnp.where(half, first, pltpu.roll(second, 64, 1))
            gsend[2 * side + 1, q] = jnp.where(half, pltpu.roll(first, 64, 1), second)
    targets = (
        (lax.rem(row + 1, n_row), col),
        (lax.rem(row + n_row - 1, n_row), col),
        (row, lax.rem(col + 1, n_col)),
        (row, lax.rem(col + n_col - 1, n_col)),
    )
    ghost_copies = [
        pltpu.make_async_remote_copy(
            src_ref=gsend.at[d],
            dst_ref=grecv.at[d],
            send_sem=gs_sem.at[d],
            recv_sem=gr_sem.at[d],
            device_id=targets[d],
            device_id_type=MESH,
        )
        for d in range(4)
    ]
    for copy in ghost_copies:
        copy.start()

    for first in range(0, QUANT, 3):
        for i, total in enumerate(star_block(turned, first)):
            p = first + i
            integ[p] = dofs[p * BASIS:(p + 1) * BASIS, :] + 0.25 * total

    def flux_block(j, side, first, read):
        totals = [None] * 3
        for q in range(QUANT):
            value = read(q)
            for i in range(3):
                r = ((j * 2 + side) * QUANT + first + i) * QUANT + q
                term = flux[r:r + 1, :] * value
                totals[i] = term if totals[i] is None else totals[i] + term
        return totals

    for j in range(4):
        for first in range(0, QUANT, 3):
            for i, total in enumerate(flux_block(j, 0, first, lambda q: xs[q, 32 * j:32 * j + 24, :])):
                comb[first + i, 24 * j:24 * j + 24, :] = total

    square_e = (elems, elems)
    for j in range(4):
        seen = nbr[j:j + 1, :]
        key = jnp.where(seen < 4 * elems, seen & (elems - 1), -1)
        glb[j] = nn(ihl[...], ones_at(iota(square_e, 0) == key)).astype(BF)

    exchange_wait(qsend, qrecv, q_sem, loc_sem.at[0])
    for k in range(2):
        item = qrecv[:, 64 * k:64 * k + 1].astype(jnp.int32) - 1
        ohk[k * devices:(k + 1) * devices, :] = ones_at(iota((devices, 4 * elems), 1) == item)

    inside = (row > 0, row < n_row - 1, col > 0, col < n_col - 1)
    for copy in ghost_copies:
        copy.wait_recv()
    for side in range(2):
        lanes = slice(side * 128, side * 128 + 128)
        for q in range(5):
            first = jnp.where(inside[2 * side], grecv[2 * side, q], 0.0)
            second = jnp.where(inside[2 * side + 1], grecv[2 * side + 1, q], 0.0)
            halves = [(q, jnp.where(half, first, pltpu.roll(second, 64, 1)))]
            if q < 4:
                halves.append((q + 5, jnp.where(half, pltpu.roll(first, 64, 1), second)))
            for quant, value in halves:
                high, low = split(padded(value))
                block = Q_ORDER.index(quant) * 128
                gtab[block:block + 64, lanes] = high
                gtab[block + 64:block + 128, lanes] = low

    def neighbours(j, start, stop):
        seen = nbr[j:j + 1, :]
        key = jnp.where(seen < 4 * elems, -1, seen & (elems - 1))
        face = lax.shift_right_logical(seen, 8) & 3
        code = ocode[j:j + 1, :]
        got = nn(gtab[start:stop, :], ones_at(iota(square_e, 0) == key)).astype(BF) + glb[j, start:stop, :]
        for block in range(start // 128, stop // 128):
            at = block * 128 - start
            high, low = got[at:at + 64], got[at + 64:at + 128]
            traces = nn(wp[...], jnp.concatenate([high, high, low], axis=0))
            value = traces[0:32]
            for f in range(1, 4):
                value = jnp.where(face == f, traces[32 * f:32 * f + 32], value)
            turns = nn(wo[...], stacked(value))
            value = turns[0:24]
            for o in range(1, 3):
                value = jnp.where(code == o, turns[24 * o:24 * o + 24], value)
            nvals[j, Q_ORDER[block]] = value

    fvals[...] = jnp.zeros_like(fvals)
    for j in range(4):
        neighbours(j, 0, HEAD)
        lanes = slice(j * elems, (j + 1) * elems)
        x0, x3, x6 = (xs[q, 32 * j:32 * j + 24, :] for q in (0, 3, 6))
        n0, n3, n6 = (nvals[j, q] for q in (0, 3, 6))
        fvals[0:24, lanes] = 0.5 * (x3 + n3) + 0.5 * (x6 - n6)
        fvals[24:48, lanes] = 0.5 * (x0 + n0)

    high, low = split(fvals[...])
    blank = jnp.zeros_like(high)
    answers = jnp.zeros((devices, 128), F32)
    for k in range(2):
        rows_k = ohk[k * devices:(k + 1) * devices, :]
        for part in (high, low):
            answers = answers + nt(rows_k, jnp.concatenate([part, blank] if k == 0 else [blank, part], axis=0))
    asend[...] = answers
    exchange_start(asend, arecv, a_sem, loc_sem.at[1])

    for j in range(4):
        neighbours(j, HEAD, 9 * 128)
    for j in range(4):
        for first in range(0, QUANT, 3):
            for i, total in enumerate(flux_block(j, 1, first, lambda q: nvals[j, q])):
                spot = (first + i, slice(24 * j, 24 * j + 24))
                comb[spot[0], spot[1], :] = comb[spot[0], spot[1], :] + total

    def lifted(value):
        high, low = split(value)
        return nn(wl[...], jnp.concatenate([high, high], axis=0)) + nn(wl[:, 0:96], low)

    for p in range(QUANT):
        out[p * BASIS:(p + 1) * BASIS, :] = integ[p] + 0.25 * lifted(comb[p])

    exchange_wait(asend, arecv, a_sem, loc_sem.at[1])
    high, low = split(arecv[...])
    eye_p = eye(128, 128)
    both = mpart[0] + mpart[1]
    own = nn(nt(eye_p, high).astype(BF), both) + nn(nt(eye_p, low).astype(BF), both)
    first_slot = rank_row == 0
    shear = jnp.where(first_slot, own[0:FACE], own[64:64 + FACE])
    normal = jnp.where(first_slot, own[24:24 + FACE], own[88:88 + FACE])
    slip = friction_solve(shear, normal, sh0[...], nm0[...], stv[...], slp[...])
    slip_out[...] = slip
    tall = jnp.concatenate([slip, jnp.zeros((64 - FACE, slip.shape[1]), F32)], axis=0)
    high, low = split(tall)
    blank = jnp.zeros_like(high)
    going = jnp.zeros((devices, 128), F32)
    for k in range(2):
        for part in (high, low):
            going = going + nt(mpart[k], jnp.concatenate([part, blank] if k == 0 else [blank, part], axis=0))
    vsend[...] = going
    exchange_start(vsend, vrecv, v_sem, loc_sem.at[2])

    exchange_wait(vsend, vrecv, v_sem, loc_sem.at[2])
    high, low = split(vrecv[...])
    rows = []
    for part in (high, low):
        sides = [
            nt(ones_at(iota((24, 128), 1) == iota((24, 128), 0) + 64 * k), part) for k in range(2)
        ]
        rows.append(jnp.concatenate(sides, axis=1))
    spread = nn(jnp.concatenate(rows, axis=0).astype(BF), ohk[...])
    spread = spread[0:24] + spread[24:48]
    push = lifted(jnp.concatenate([spread[:, j * elems:(j + 1) * elems] for j in range(4)], axis=0))
    out[3 * BASIS:4 * BASIS, :] = out[3 * BASIS:4 * BASIS, :] - 0.5 * push
    out[6 * BASIS:7 * BASIS, :] = out[6 * BASIS:7 * BASIS, :] + 0.5 * push

    for copy in ghost_copies:
        copy.wait_send()
    exchange_end(qsend, q_sem)
    exchange_end(asend, a_sem)
    exchange_end(vsend, v_sem)


def solution(mesh):
    n_row, n_col = mesh.shape["row"], mesh.shape["col"]
    devices = n_row * n_col

    def per_device(dofs, star, flux, kxi, proj, lift, orient, nbr, ocode, slist, fpart, fitem, sh0, nm0, stv, slp):
        elems = dofs.shape[1]
        vmem = pl.BlockSpec(memory_space=pltpu.VMEM)
        table = pltpu.VMEM((devices, 128), F32)
        pair = pltpu.SemaphoreType.DMA((2,))
        four = pltpu.SemaphoreType.DMA((4,))
        return pl.pallas_call(
            lambda *refs: kernel(n_row, n_col, *refs),
            out_shape=(
                jax.ShapeDtypeStruct(dofs.shape, F32),
                jax.ShapeDtypeStruct(slp.shape, F32),
            ),
            in_specs=[vmem] * 16,
            out_specs=(vmem, vmem),
            scratch_shapes=[
                pltpu.VMEM((3 * BASIS, 192), BF),
                pltpu.VMEM((3 * BASIS, 192), BF),
                pltpu.VMEM((128, 192), BF),
                pltpu.VMEM((72, 96), BF),
                pltpu.VMEM((BASIS, 192), BF),
                pltpu.VMEM((2, QUANT, 3 * BASIS, elems), F32),
                pltpu.VMEM((QUANT, BASIS, elems), F32),
                pltpu.VMEM((QUANT * 128, elems), BF),
                pltpu.VMEM((QUANT, 128, elems), F32),
                pltpu.VMEM((4, QUANT * 128, elems), BF),
                pltpu.VMEM((QUANT * 128, elems), BF),
                pltpu.VMEM((4, QUANT, 24, elems), F32),
                pltpu.VMEM((QUANT, 96, elems), F32),
                pltpu.VMEM((64, 4 * elems), F32),
                pltpu.VMEM((2 * devices, 4 * elems), BF),
                pltpu.VMEM((2, devices, 128), BF),
                pltpu.VMEM((4, 5, BASIS, 128), F32),
                pltpu.VMEM((4, 5, BASIS, 128), F32),
                table, table, table, table, table, table,
                four, four, pair, pair, pair, pltpu.SemaphoreType.DMA((3,)),
            ],
            compiler_params=pltpu.CompilerParams(collective_id=0, has_side_effects=True),
        )(dofs, star, flux, kxi, proj, lift, orient, nbr, ocode, slist, fpart, fitem.reshape(1, -1), sh0, nm0, stv, slp)

    split_cols = P(None, ("row", "col"))
    placed = (
        (split_cols,) * 3
        + (P(),) * 4
        + (split_cols,) * 3
        + (P(("row", "col"), None), P(("row", "col")))
        + (split_cols,) * 4
    )
    return jax.shard_map(
        per_device, mesh=mesh, in_specs=placed, out_specs=(split_cols, split_cols), check_vma=False
    )
```

```python
import jax
import jax.numpy as jnp
from jax import lax
from jax.experimental import pallas as pl
from jax.experimental.pallas import tpu as pltpu
from jax.sharding import PartitionSpec as P

QUANT = 9
BASIS = 56
FACE = 21
ORDER = 6
NEWTON_ITERS = 3
TIME_STEP = 2.0
FRIC_A = 0.5
MESH = pl.DeviceIdType.MESH
LOGICAL = pl.DeviceIdType.LOGICAL
BF = jnp.bfloat16
F32 = jnp.float32

Q_ORDER = (0, 3, 6, 1, 2, 4, 5, 7, 8)
HEAD = 3 * 128


def iota(shape, dim):
    return lax.broadcasted_iota(jnp.int32, shape, dim)


def ones_at(mask):
    return jnp.where(mask, 1.0, 0.0).astype(BF)


def nn(a, b):
    return jnp.dot(a, b, preferred_element_type=F32)


def nt(a, b):
    return lax.dot_general(a, b, (((1,), (1,)), ((), ())), preferred_element_type=F32)


def split(x):
    high = x.astype(BF)
    return high, (x - high.astype(F32)).astype(BF)


def eye(rows, cols):
    return ones_at(iota((rows, cols), 0) == iota((rows, cols), 1))


def place(rows, cols, offsets):
    delta = iota((rows, cols), 1) - iota((rows, cols), 0)
    mask = delta == offsets[0]
    for offset in offsets[1:]:
        mask = mask | (delta == offset)
    return ones_at(mask)


def padded(x):
    return jnp.concatenate([x, jnp.zeros((8, x.shape[1]), F32)], axis=0)


def stacked(x):
    high, low = split(x)
    return jnp.concatenate([high, high, low], axis=0)


def inverse_sinh(value):
    magnitude = jnp.abs(value)
    squared = magnitude * magnitude
    positive = jnp.log1p(magnitude + squared / (1.0 + jnp.sqrt(1.0 + squared)))
    return jnp.where(value < 0.0, -positive, positive)


def friction_solve(shear, normal, shear_init, normal_init, state_var, slip_prev):
    shear_total = shear_init + shear
    normal_eff = normal_init * (1.0 + 0.5 * jnp.tanh(normal))
    growth = jnp.exp(state_var / FRIC_A) * 0.5
    slip_now = slip_prev
    for _ in range(NEWTON_ITERS):
        scaled = growth * slip_now
        misfit = shear_total - slip_now - FRIC_A * normal_eff * inverse_sinh(scaled)
        slope_val = -1.0 - FRIC_A * normal_eff * growth / jnp.sqrt(1.0 + scaled * scaled)
        slip_now = slip_now - misfit / slope_val
    return slip_now


def kernel(
    n_row, n_col,
    dofs, star, flux, kxi, proj, lift, orient, nbr, ocode, slist, fpart, fitem, sh0, nm0, stv, slp,
    out, slip_out,
    wk, wv, wp, wo, w12, tall, wl, adv, integ, ihl, xs, glb, gtab, nvals, comb, fvals, ohk, mpart,
    gsend, grecv, qsend, qrecv, asend, arecv, vsend, vrecv,
    gs_sem, gr_sem, q_sem, a_sem, v_sem, loc_sem,
):
    devices = n_row * n_col
    row, col = lax.axis_index("row"), lax.axis_index("col")
    me = row * n_col + col

    barrier = pltpu.get_barrier_semaphore()

    def ring(at, size, scale):
        return [lax.rem(at + step, size) * scale for step in range(size)]

    across = ring(row, n_row, n_col)
    deep = ring(col // 8, 4, 8)
    wide = ring(lax.rem(col, 8) // 2, 4, 2)
    core = ring(lax.rem(col, 2), 2, 1)
    hops = (0, 1, 2, 1)
    steps = [(y, z, x, c) for y in range(4) for z in range(4) for x in range(4) for c in range(2)][1:]
    steps.sort(key=lambda at: -(hops[at[0]] + hops[at[1]] + hops[at[2]]))

    def partner(at):
        return (across[at[0]] + deep[at[1]]) + (wide[at[2]] + core[at[3]])

    for at in steps:
        pl.semaphore_signal(barrier, inc=1, device_id=partner(at), device_id_type=LOGICAL)

    def exchange_start(send, recv, sem, local_sem):
        for at in steps:
            p = partner(at)
            pltpu.make_async_remote_copy(
                src_ref=send.at[pl.ds(p, 1)],
                dst_ref=recv.at[pl.ds(me, 1)],
                send_sem=sem.at[0],
                recv_sem=sem.at[1],
                device_id=p,
                device_id_type=LOGICAL,
            ).start()
        pltpu.make_async_copy(send.at[pl.ds(me, 1)], recv.at[pl.ds(me, 1)], local_sem).start()

    def exchange_wait(send, recv, sem, local_sem):
        part = pl.ds(0, devices - 1)
        pltpu.make_async_copy(recv.at[part], recv.at[part], sem.at[1]).wait()
        pltpu.make_async_copy(send.at[pl.ds(me, 1)], recv.at[pl.ds(me, 1)], local_sem).wait()

    def exchange_end(send, sem):
        part = pl.ds(0, devices - 1)
        pltpu.make_async_copy(send.at[part], send.at[part], sem.at[0]).wait()

    at_high, at_low = place(BASIS, 192, (0, 128)), place(BASIS, 192, (64,))
    eye_b = eye(BASIS, BASIS)
    back, forth = [], []
    for d in range(3):
        high, low = split(kxi[d])
        forth.append(nn(high, at_high) + nn(low, at_low))
        back.append(nn(nt(eye_b, high).astype(BF), at_high) + nn(nt(eye_b, low).astype(BF), at_low))
    wk[...] = jnp.concatenate(back, axis=0).astype(BF)
    wv[...] = jnp.concatenate(forth, axis=0).astype(BF)
    flat = 4 * FACE
    for g in range(FACE):
        tall[0, 4 * g:4 * g + 4, :] = proj[g]
        tall[1, 4 * g:4 * g + 4, :] = lift[g]
    shape = (128, flat)
    order = ones_at((iota(shape, 0) // 32 + 4 * lax.rem(iota(shape, 0), 32)) == iota(shape, 1))
    high, low = split(tall[0])
    proj_high, proj_low = nn(order, high).astype(BF), nn(order, low).astype(BF)
    wp[...] = (nn(proj_high, at_high) + nn(proj_low, at_low)).astype(BF)
    rows = []
    pick_g = eye(24, FACE)
    turn_high, turn_low = place(FACE, 96, (0, 64)), place(FACE, 96, (32,))
    for o in range(3):
        high, low = split(orient[o])
        rows.append(nn(nt(pick_g, high).astype(BF), turn_high) + nn(nt(pick_g, low).astype(BF), turn_low))
    turn = jnp.concatenate(rows, axis=0).astype(BF)
    for j in range(4):
        own_rows = slice(32 * j, 32 * j + 32)
        both = jnp.concatenate([proj_high[own_rows], proj_high[own_rows], proj_low[own_rows]], axis=0)
        high, low = split(nn(turn, both))
        wo[72 * j:72 * j + 72, :] = nn(high, at_high) + nn(low, at_low)
    w12[...] = wo[...].astype(BF)
    shape = (flat, 192)
    spot = 24 * lax.rem(iota(shape, 0), 4) + iota(shape, 0) // 4
    high, low = split(tall[1])
    table = nn(nt(eye_b, high).astype(BF), ones_at(iota(shape, 1) == spot))
    table = table + nn(nt(eye_b, low).astype(BF), ones_at(iota(shape, 1) == spot + 96))
    wl[...] = table.astype(BF)

    square = (devices, fitem.shape[1])
    part_row = fpart[...]
    wide_part = jnp.sum(jnp.where(iota(square, 0) == iota(square, 1), part_row, 0), axis=1, keepdims=True)
    earlier = (wide_part == part_row) & (iota(square, 0) < iota(square, 1))
    rank_row = jnp.sum(jnp.where(earlier, 1, 0), axis=0, keepdims=True)
    names = iota(square, 0) == part_row
    mpart[0] = ones_at(names & (rank_row == 0))
    mpart[1] = ones_at(names & (rank_row == 1))
    code_row = (fitem[...] + 1).astype(F32)
    asked = [
        jnp.sum(jnp.where(names & (rank_row == k), code_row, 0.0), axis=1, keepdims=True) for k in range(2)
    ]
    low_lane = iota((devices, 128), 1) < 64
    qsend[...] = jnp.where(low_lane, asked[0], asked[1])

    def put(weights, value, target, q):
        target[q] = nn(weights[...], stacked(padded(value)))

    for q in range(QUANT):
        start = dofs[q * BASIS:(q + 1) * BASIS, :]
        integ[q] = TIME_STEP * start
        put(wk, start, adv.at[0], q)

    def star_block(source, first):
        sides = []
        for lanes in (slice(0, 128), slice(128, 256)):
            totals = [None] * 3
            for q in range(QUANT):
                for d in range(3):
                    value = source[q, d * BASIS:(d + 1) * BASIS, lanes]
                    for i in range(3):
                        r = (d * QUANT + first + i) * QUANT + q
                        term = star[r:r + 1, lanes] * value
                        totals[i] = term if totals[i] is None else totals[i] + term
            sides.append(totals)
        return [jnp.concatenate([left, right], axis=1) for left, right in zip(*sides)]

    factor = TIME_STEP
    for k in range(1, ORDER):
        if k == 3:
            pl.semaphore_wait(barrier, devices - 1)
            exchange_start(qsend, qrecv, q_sem, loc_sem.at[0])
        factor = factor * TIME_STEP / (k + 1)
        source, target = adv.at[(k - 1) % 2], adv.at[k % 2]
        for first in range(0, QUANT, 3):
            for i, total in enumerate(star_block(source, first)):
                p = first + i
                if k < ORDER - 1:
                    integ[p] = integ[p] + factor * total
                    put(wk, total, target, p)
                else:
                    high, low = split(padded(integ[p] + factor * total))
                    block = Q_ORDER.index(p) * 128
                    ihl[block:block + 64, :] = high
                    ihl[block + 64:block + 128, :] = low
                    both = jnp.concatenate([high, high, low], axis=0)
                    target[p] = nn(wv[...], both)
                    xs[p] = nn(wp[...], both)
    turned = adv.at[(ORDER - 1) % 2]

    small = slist.shape[1]
    spread = ones_at(lax.rem(iota((small, 4 * small), 1), small) == iota((small, 4 * small), 0))
    listed = nn(slist[...].astype(F32).astype(BF), spread)
    listed = jnp.sum(
        jnp.where(iota((4, 4 * small), 1) // small == iota((4, 4 * small), 0), listed, 0.0), axis=0, keepdims=True
    ).astype(jnp.int32)
    elems = dofs.shape[1]
    picked = nn(ihl[...], ones_at(iota((elems, 4 * small), 0) == listed))
    half = iota((BASIS, 128), 1) < 64

    def pick(q, side):
        block = Q_ORDER.index(q) * 128
        lanes = slice(side * 128, side * 128 + 128)
        return picked[block:block + BASIS, lanes] + picked[block + 64:block + 64 + BASIS, lanes]

    for side in range(2):
        for q in range(5):
            first = pick(q, side)
            second = pick(q + 5, side) if q < 4 else first
            gsend[2 * side, q] = jnp.where(half, first, pltpu.roll(second, 64, 1))
            gsend[2 * side + 1, q] = jnp.where(half, pltpu.roll(first, 64, 1), second)
    targets = (
        (lax.rem(row + 1, n_row), col),
        (lax.rem(row + n_row - 1, n_row), col),
        (row, lax.rem(col + 1, n_col)),
        (row, lax.rem(col + n_col - 1, n_col)),
    )
    ghost_copies = [
        pltpu.make_async_remote_copy(
            src_ref=gsend.at[d],
            dst_ref=grecv.at[d],
            send_sem=gs_sem.at[d],
            recv_sem=gr_sem.at[d],
            device_id=targets[d],
            device_id_type=MESH,
        )
        for d in range(4)
    ]
    for copy in ghost_copies:
        copy.start()

    for first in range(0, QUANT, 3):
        for i, total in enumerate(star_block(turned, first)):
            p = first + i
            integ[p] = dofs[p * BASIS:(p + 1) * BASIS, :] + 0.25 * total

    def flux_block(j, side, first, read):
        totals = [None] * 3
        for q in range(QUANT):
            value = read(q)
            for i in range(3):
                r = ((j * 2 + side) * QUANT + first + i) * QUANT + q
                term = flux[r:r + 1, :] * value
                totals[i] = term if totals[i] is None else totals[i] + term
        return totals

    for j in range(4):
        for first in range(0, QUANT, 3):
            for i, total in enumerate(flux_block(j, 0, first, lambda q: xs[q, 32 * j:32 * j + 24, :])):
                comb[first + i, 24 * j:24 * j + 24, :] = total

    square_e = (elems, elems)
    for j in range(4):
        seen = nbr[j:j + 1, :]
        key = jnp.where(seen < 4 * elems, seen & (elems - 1), -1)
        glb[j] = nn(ihl[...], ones_at(iota(square_e, 0) == key)).astype(BF)

    exchange_wait(qsend, qrecv, q_sem, loc_sem.at[0])
    for k in range(2):
        item = qrecv[:, 64 * k:64 * k + 1].astype(jnp.int32) - 1
        ohk[k * devices:(k + 1) * devices, :] = ones_at(iota((devices, 4 * elems), 1) == item)

    inside = (row > 0, row < n_row - 1, col > 0, col < n_col - 1)
    for copy in ghost_copies:
        copy.wait_recv()
    for side in range(2):
        lanes = slice(side * 128, side * 128 + 128)
        for q in range(5):
            first = jnp.where(inside[2 * side], grecv[2 * side, q], 0.0)
            second = jnp.where(inside[2 * side + 1], grecv[2 * side + 1, q], 0.0)
            halves = [(q, jnp.where(half, first, pltpu.roll(second, 64, 1)))]
            if q < 4:
                halves.append((q + 5, jnp.where(half, pltpu.roll(first, 64, 1), second)))
            for quant, value in halves:
                high, low = split(padded(value))
                block = Q_ORDER.index(quant) * 128
                gtab[block:block + 64, lanes] = high
                gtab[block + 64:block + 128, lanes] = low

    def neighbours(j, start, stop):
        seen = nbr[j:j + 1, :]
        key = jnp.where(seen < 4 * elems, -1, seen & (elems - 1))
        code = 3 * (lax.shift_right_logical(seen, 8) & 3) + ocode[j:j + 1, :]
        got = nn(gtab[start:stop, :], ones_at(iota(square_e, 0) == key)).astype(BF) + glb[j, start:stop, :]
        for block in range(start // 128, stop // 128):
            at = block * 128 - start
            high, low = got[at:at + 64], got[at + 64:at + 128]
            turns = nn(w12[...], jnp.concatenate([high, high, low], axis=0))
            value = turns[0:24]
            for c in range(1, 12):
                value = jnp.where(code == c, turns[24 * c:24 * c + 24], value)
            nvals[j, Q_ORDER[block]] = value

    fvals[...] = jnp.zeros_like(fvals)
    for j in range(4):
        neighbours(j, 0, HEAD)
        lanes = slice(j * elems, (j + 1) * elems)
        x0, x3, x6 = (xs[q, 32 * j:32 * j + 24, :] for q in (0, 3, 6))
        n0, n3, n6 = (nvals[j, q] for q in (0, 3, 6))
        fvals[0:24, lanes] = 0.5 * (x3 + n3) + 0.5 * (x6 - n6)
        fvals[24:48, lanes] = 0.5 * (x0 + n0)

    high, low = split(fvals[...])
    blank = jnp.zeros_like(high)
    answers = jnp.zeros((devices, 128), F32)
    for k in range(2):
        rows_k = ohk[k * devices:(k + 1) * devices, :]
        for part in (high, low):
            answers = answers + nt(rows_k, jnp.concatenate([part, blank] if k == 0 else [blank, part], axis=0))
    asend[...] = answers
    exchange_start(asend, arecv, a_sem, loc_sem.at[1])

    for j in range(4):
        neighbours(j, HEAD, 9 * 128)
    for j in range(4):
        for first in range(0, QUANT, 3):
            for i, total in enumerate(flux_block(j, 1, first, lambda q: nvals[j, q])):
                spot = (first + i, slice(24 * j, 24 * j + 24))
                comb[spot[0], spot[1], :] = comb[spot[0], spot[1], :] + total

    def lifted(value):
        high, low = split(value)
        return nn(wl[...], jnp.concatenate([high, high], axis=0)) + nn(wl[:, 0:96], low)

    for p in range(QUANT):
        out[p * BASIS:(p + 1) * BASIS, :] = integ[p] + 0.25 * lifted(comb[p])

    exchange_wait(asend, arecv, a_sem, loc_sem.at[1])
    high, low = split(arecv[...])
    eye_p = eye(128, 128)
    both = mpart[0] + mpart[1]
    own = nn(nt(eye_p, high).astype(BF), both) + nn(nt(eye_p, low).astype(BF), both)
    first_slot = rank_row == 0
    shear = jnp.where(first_slot, own[0:FACE], own[64:64 + FACE])
    normal = jnp.where(first_slot, own[24:24 + FACE], own[88:88 + FACE])
    slip = friction_solve(shear, normal, sh0[...], nm0[...], stv[...], slp[...])
    slip_out[...] = slip
    column = jnp.concatenate([slip, jnp.zeros((64 - FACE, slip.shape[1]), F32)], axis=0)
    high, low = split(column)
    blank = jnp.zeros_like(high)
    going = jnp.zeros((devices, 128), F32)
    for k in range(2):
        for part in (high, low):
            going = going + nt(mpart[k], jnp.concatenate([part, blank] if k == 0 else [blank, part], axis=0))
    vsend[...] = going
    exchange_start(vsend, vrecv, v_sem, loc_sem.at[2])

    exchange_wait(vsend, vrecv, v_sem, loc_sem.at[2])
    high, low = split(vrecv[...])
    rows = []
    for part in (high, low):
        sides = [
            nt(ones_at(iota((24, 128), 1) == iota((24, 128), 0) + 64 * k), part) for k in range(2)
        ]
        rows.append(jnp.concatenate(sides, axis=1))
    spread = nn(jnp.concatenate(rows, axis=0).astype(BF), ohk[...])
    spread = spread[0:24] + spread[24:48]
    push = lifted(jnp.concatenate([spread[:, j * elems:(j + 1) * elems] for j in range(4)], axis=0))
    out[3 * BASIS:4 * BASIS, :] = out[3 * BASIS:4 * BASIS, :] - 0.5 * push
    out[6 * BASIS:7 * BASIS, :] = out[6 * BASIS:7 * BASIS, :] + 0.5 * push

    for copy in ghost_copies:
        copy.wait_send()
    exchange_end(qsend, q_sem)
    exchange_end(asend, a_sem)
    exchange_end(vsend, v_sem)


def solution(mesh):
    n_row, n_col = mesh.shape["row"], mesh.shape["col"]
    devices = n_row * n_col

    def per_device(dofs, star, flux, kxi, proj, lift, orient, nbr, ocode, slist, fpart, fitem, sh0, nm0, stv, slp):
        elems = dofs.shape[1]
        vmem = pl.BlockSpec(memory_space=pltpu.VMEM)
        table = pltpu.VMEM((devices, 128), F32)
        pair = pltpu.SemaphoreType.DMA((2,))
        four = pltpu.SemaphoreType.DMA((4,))
        return pl.pallas_call(
            lambda *refs: kernel(n_row, n_col, *refs),
            out_shape=(
                jax.ShapeDtypeStruct(dofs.shape, F32),
                jax.ShapeDtypeStruct(slp.shape, F32),
            ),
            in_specs=[vmem] * 16,
            out_specs=(vmem, vmem),
            scratch_shapes=[
                pltpu.VMEM((3 * BASIS, 192), BF),
                pltpu.VMEM((3 * BASIS, 192), BF),
                pltpu.VMEM((128, 192), BF),
                pltpu.VMEM((288, 192), F32),
                pltpu.VMEM((288, 192), BF),
                pltpu.VMEM((2, 4 * FACE, BASIS), F32),
                pltpu.VMEM((BASIS, 192), BF),
                pltpu.VMEM((2, QUANT, 3 * BASIS, elems), F32),
                pltpu.VMEM((QUANT, BASIS, elems), F32),
                pltpu.VMEM((QUANT * 128, elems), BF),
                pltpu.VMEM((QUANT, 128, elems), F32),
                pltpu.VMEM((4, QUANT * 128, elems), BF),
                pltpu.VMEM((QUANT * 128, elems), BF),
                pltpu.VMEM((4, QUANT, 24, elems), F32),
                pltpu.VMEM((QUANT, 96, elems), F32),
                pltpu.VMEM((64, 4 * elems), F32),
                pltpu.VMEM((2 * devices, 4 * elems), BF),
                pltpu.VMEM((2, devices, 128), BF),
                pltpu.VMEM((4, 5, BASIS, 128), F32),
                pltpu.VMEM((4, 5, BASIS, 128), F32),
                table, table, table, table, table, table,
                four, four, pair, pair, pair, pltpu.SemaphoreType.DMA((3,)),
            ],
            compiler_params=pltpu.CompilerParams(collective_id=0, has_side_effects=True),
        )(
            dofs, star, flux, kxi, jnp.transpose(proj, (2, 0, 1)), jnp.transpose(lift, (1, 0, 2)), orient,
            nbr, ocode, slist, fpart.reshape(1, -1), fitem.reshape(1, -1), sh0, nm0, stv, slp,
        )

    split_cols = P(None, ("row", "col"))
    placed = (
        (split_cols,) * 3
        + (P(),) * 4
        + (split_cols,) * 3
        + (P(("row", "col"), None), P(("row", "col")))
        + (split_cols,) * 4
    )
    return jax.shard_map(
        per_device, mesh=mesh, in_specs=placed, out_specs=(split_cols, split_cols), check_vma=False
    )
```

```python
import jax
import jax.numpy as jnp
from jax import lax
from jax.experimental import pallas as pl
from jax.experimental.pallas import tpu as pltpu
from jax.sharding import PartitionSpec as P

QUANT = 9
BASIS = 56
FACE = 21
ORDER = 6
NEWTON_ITERS = 3
TIME_STEP = 2.0
FRIC_A = 0.5
MESH = pl.DeviceIdType.MESH
LOGICAL = pl.DeviceIdType.LOGICAL
BF = jnp.bfloat16
F32 = jnp.float32

Q_ORDER = (0, 3, 6, 1, 2, 4, 5, 7, 8)
GROUPS = (Q_ORDER[0:3], Q_ORDER[3:6], Q_ORDER[6:9])
HEAD = 3 * 128
HEAD_PAIRS = ((0, 3), (6, 6))
REST_PAIRS = ((1, 2), (4, 5), (7, 8))
AT_SHEAR, AT_NORMAL, AT_STATE, AT_SLIP, AT_ITEM = 0, 24, 48, 72, 96


def iota(shape, dim):
    return lax.broadcasted_iota(jnp.int32, shape, dim)


def ones_at(mask):
    return jnp.where(mask, 1.0, 0.0).astype(BF)


def nn(a, b):
    return jnp.dot(a, b, preferred_element_type=F32)


def nt(a, b):
    return lax.dot_general(a, b, (((1,), (1,)), ((), ())), preferred_element_type=F32)


def split(x):
    high = x.astype(BF)
    return high, (x - high.astype(F32)).astype(BF)


def eye(rows, cols):
    return ones_at(iota((rows, cols), 0) == iota((rows, cols), 1))


def place(rows, cols, offsets):
    delta = iota((rows, cols), 1) - iota((rows, cols), 0)
    mask = delta == offsets[0]
    for offset in offsets[1:]:
        mask = mask | (delta == offset)
    return ones_at(mask)


def padded(x):
    return jnp.concatenate([x, jnp.zeros((8, x.shape[1]), F32)], axis=0)


def stacked(x):
    high, low = split(x)
    return jnp.concatenate([high, high, low], axis=0)


def inverse_sinh(value):
    magnitude = jnp.abs(value)
    squared = magnitude * magnitude
    positive = jnp.log1p(magnitude + squared / (1.0 + jnp.sqrt(1.0 + squared)))
    return jnp.where(value < 0.0, -positive, positive)


def friction_solve(shear, normal, shear_init, normal_init, state_var, slip_prev):
    shear_total = shear_init + shear
    normal_eff = normal_init * (1.0 + 0.5 * jnp.tanh(normal))
    growth = jnp.exp(state_var / FRIC_A) * 0.5
    slip_now = slip_prev
    for _ in range(NEWTON_ITERS):
        scaled = growth * slip_now
        misfit = shear_total - slip_now - FRIC_A * normal_eff * inverse_sinh(scaled)
        slope_val = -1.0 - FRIC_A * normal_eff * growth / jnp.sqrt(1.0 + scaled * scaled)
        slip_now = slip_now - misfit / slope_val
    return slip_now


def kernel(
    n_row, n_col,
    dofs_in, star_in, flux_in, kxi, proj, lift, orient, nbr, ocode, slist, fpart, fitem, sh0, nm0, stv, slp,
    out, slip_out,
    dofs, star, flux, result,
    wk, wv, wp, wo, w12, tall, wl, adv, integ, ihl, xs, glb, gtab, nvals, comb, fvals, oht, params,
    gsend, grecv, hsend, hrecv, qsend, qrecv, vsend, vrecv,
    gs_sem, gr_sem, hs_sem, hr_sem, q_sem, v_sem, loc_sem, in_sem, out_sem,
):
    devices = n_row * n_col
    loads = [
        pltpu.make_async_copy(source, target, in_sem.at[n])
        for n, (source, target) in enumerate(((dofs_in, dofs), (star_in, star), (flux_in, flux)))
    ]
    for load in loads:
        load.start()
    row, col = lax.axis_index("row"), lax.axis_index("col")
    me = row * n_col + col

    barrier = pltpu.get_barrier_semaphore()

    def ring(at, size, scale):
        return [lax.rem(at + step, size) * scale for step in range(size)]

    across = ring(row, n_row, n_col)
    deep = ring(col // 8, 4, 8)
    wide = ring(lax.rem(col, 8) // 2, 4, 2)
    core = ring(lax.rem(col, 2), 2, 1)
    hops = (0, 1, 2, 1)
    steps = [(y, z, x, c) for y in range(4) for z in range(4) for x in range(4) for c in range(2)][1:]
    steps.sort(key=lambda at: -(hops[at[0]] + hops[at[1]] + hops[at[2]]))

    def partner(at):
        return (across[at[0]] + deep[at[1]]) + (wide[at[2]] + core[at[3]])

    for at in steps:
        pl.semaphore_signal(barrier, inc=1, device_id=partner(at), device_id_type=LOGICAL)

    def own_copy(n, send, recv, local_sem):
        mine = pl.ds(n * me, n)
        return pltpu.make_async_copy(send.at[mine], recv.at[mine], local_sem)

    def exchange_start(n, send, recv, sem, local_sem):
        for at in steps:
            p = partner(at)
            pltpu.make_async_remote_copy(
                src_ref=send.at[pl.ds(n * p, n)],
                dst_ref=recv.at[pl.ds(n * me, n)],
                send_sem=sem.at[0],
                recv_sem=sem.at[1],
                device_id=p,
                device_id_type=LOGICAL,
            ).start()
        own_copy(n, send, recv, local_sem).start()

    def exchange_wait(n, send, recv, sem, local_sem):
        part = pl.ds(0, n * (devices - 1))
        pltpu.make_async_copy(recv.at[part], recv.at[part], sem.at[1]).wait()
        own_copy(n, send, recv, local_sem).wait()

    def exchange_end(n, send, sem):
        part = pl.ds(0, n * (devices - 1))
        pltpu.make_async_copy(send.at[part], send.at[part], sem.at[0]).wait()

    at_high, at_low = place(BASIS, 192, (0, 128)), place(BASIS, 192, (64,))
    eye_b = eye(BASIS, BASIS)
    back, forth = [], []
    for d in range(3):
        high, low = split(kxi[d])
        forth.append(nn(high, at_high) + nn(low, at_low))
        back.append(nn(nt(eye_b, high).astype(BF), at_high) + nn(nt(eye_b, low).astype(BF), at_low))
    wk[...] = jnp.concatenate(back, axis=0).astype(BF)
    wv[...] = jnp.concatenate(forth, axis=0).astype(BF)
    flat = 4 * FACE
    for g in range(FACE):
        tall[0, 4 * g:4 * g + 4, :] = proj[g]
        tall[1, 4 * g:4 * g + 4, :] = lift[g]
    shape = (128, flat)
    order = ones_at((iota(shape, 0) // 32 + 4 * lax.rem(iota(shape, 0), 32)) == iota(shape, 1))
    high, low = split(tall[0])
    proj_high, proj_low = nn(order, high).astype(BF), nn(order, low).astype(BF)
    wp[...] = (nn(proj_high, at_high) + nn(proj_low, at_low)).astype(BF)
    rows = []
    pick_g = eye(24, FACE)
    turn_high, turn_low = place(FACE, 96, (0, 64)), place(FACE, 96, (32,))
    for o in range(3):
        high, low = split(orient[o])
        rows.append(nn(nt(pick_g, high).astype(BF), turn_high) + nn(nt(pick_g, low).astype(BF), turn_low))
    turn = jnp.concatenate(rows, axis=0).astype(BF)
    for j in range(4):
        own_rows = slice(32 * j, 32 * j + 32)
        both = jnp.concatenate([proj_high[own_rows], proj_high[own_rows], proj_low[own_rows]], axis=0)
        high, low = split(nn(turn, both))
        wo[72 * j:72 * j + 72, :] = nn(high, at_high) + nn(low, at_low)
    w12[...] = wo[...].astype(BF)
    shape = (flat, 192)
    spot = 24 * lax.rem(iota(shape, 0), 4) + iota(shape, 0) // 4
    high, low = split(tall[1])
    table = nn(nt(eye_b, high).astype(BF), ones_at(iota(shape, 1) == spot))
    table = table + nn(nt(eye_b, low).astype(BF), ones_at(iota(shape, 1) == spot + 96))
    wl[...] = table.astype(BF)

    square = (devices, fitem.shape[1])
    part_row = fpart[...]
    wide_part = jnp.sum(jnp.where(iota(square, 0) == iota(square, 1), part_row, 0), axis=1, keepdims=True)
    earlier = (wide_part == part_row) & (iota(square, 0) < iota(square, 1))
    rank_row = jnp.sum(jnp.where(earlier, 1, 0), axis=0, keepdims=True)
    tall_square = (2 * devices, fitem.shape[1])
    slot_of = ones_at(iota(tall_square, 0) == 2 * part_row + rank_row)
    params[...] = jnp.zeros_like(params)
    for at, table in ((AT_SHEAR, sh0), (AT_NORMAL, nm0), (AT_STATE, stv), (AT_SLIP, slp)):
        params[at:at + FACE, :] = table[...]
    params[AT_ITEM:AT_ITEM + 1, :] = (fitem[...] + 1).astype(F32)
    high, low = split(params[...])
    qsend[...] = nt(slot_of, high) + nt(slot_of, low)

    def put(weights, value, target, q):
        target[q] = nn(weights[...], stacked(padded(value)))

    loads[0].wait()
    loads[1].wait()
    for q in Q_ORDER:
        start = dofs[q * BASIS:(q + 1) * BASIS, :]
        integ[q] = TIME_STEP * start
        put(wk, start, adv.at[0], q)

    def star_block(source, group):
        sides = []
        for lanes in (slice(0, 128), slice(128, 256)):
            totals = [None] * 3
            for q in Q_ORDER:
                for d in range(3):
                    value = source[q, d * BASIS:(d + 1) * BASIS, lanes]
                    for i, p in enumerate(group):
                        r = (d * QUANT + p) * QUANT + q
                        term = star[r:r + 1, lanes] * value
                        totals[i] = term if totals[i] is None else totals[i] + term
            sides.append(totals)
        return [(p, jnp.concatenate([left, right], axis=1)) for p, left, right in zip(group, *sides)]

    factor = TIME_STEP
    for k in range(1, ORDER - 1):
        if k == 3:
            pl.semaphore_wait(barrier, devices - 1)
            exchange_start(2, qsend, qrecv, q_sem, loc_sem.at[0])
        factor = factor * TIME_STEP / (k + 1)
        source, target = adv.at[(k - 1) % 2], adv.at[k % 2]
        for group in GROUPS:
            for p, total in star_block(source, group):
                integ[p] = integ[p] + factor * total
                put(wk, total, target, p)
    factor = factor * TIME_STEP / ORDER
    source, turned = adv.at[(ORDER - 2) % 2], adv.at[(ORDER - 1) % 2]

    small = slist.shape[1]
    elems = dofs.shape[1]
    spread = ones_at(lax.rem(iota((small, 4 * small), 1), small) == iota((small, 4 * small), 0))
    listed = nn(slist[...].astype(F32).astype(BF), spread)
    listed = jnp.sum(
        jnp.where(iota((4, 4 * small), 1) // small == iota((4, 4 * small), 0), listed, 0.0), axis=0, keepdims=True
    ).astype(jnp.int32)
    half = iota((BASIS, 128), 1) < 64
    targets = (
        lax.rem(row + 1, n_row) * n_col + col,
        lax.rem(row + n_row - 1, n_row) * n_col + col,
        row * n_col + lax.rem(col + 1, n_col),
        row * n_col + lax.rem(col + n_col - 1, n_col),
    )

    def ghost_copies(send, recv, send_sem, recv_sem):
        return [
            pltpu.make_async_remote_copy(
                src_ref=send.at[d],
                dst_ref=recv.at[d],
                send_sem=send_sem.at[d],
                recv_sem=recv_sem.at[d],
                device_id=targets[d],
                device_id_type=LOGICAL,
            )
            for d in range(4)
        ]

    head_copies = ghost_copies(hsend, hrecv, hs_sem, hr_sem)
    rest_copies = ghost_copies(gsend, grecv, gs_sem, gr_sem)

    def pack(send, pairs, start, stop):
        picked = nn(ihl[start:stop, :], ones_at(iota((elems, 4 * small), 0) == listed))
        for side in range(2):
            lanes = slice(side * 128, side * 128 + 128)
            for n, pair in enumerate(pairs):
                ends = []
                for q in pair:
                    at = Q_ORDER.index(q) * 128 - start
                    ends.append(picked[at:at + BASIS, lanes] + picked[at + 64:at + 64 + BASIS, lanes])
                first, second = ends
                send[2 * side, n] = jnp.where(half, first, pltpu.roll(second, 64, 1))
                send[2 * side + 1, n] = jnp.where(half, pltpu.roll(first, 64, 1), second)

    def finish(group):
        for p, total in star_block(source, group):
            high, low = split(padded(integ[p] + factor * total))
            block = Q_ORDER.index(p) * 128
            ihl[block:block + 64, :] = high
            ihl[block + 64:block + 128, :] = low

    def stacked_of(p):
        block = Q_ORDER.index(p) * 128
        high = ihl[block:block + 64, :]
        return jnp.concatenate([high, high, ihl[block + 64:block + 128, :]], axis=0)

    finish(GROUPS[0])
    pack(hsend, HEAD_PAIRS, 0, HEAD)
    for copy in head_copies:
        copy.start()
    for p in GROUPS[0]:
        xs[p] = nn(wp[...], stacked_of(p))
    finish(GROUPS[1])
    finish(GROUPS[2])
    pack(gsend, REST_PAIRS, HEAD, 9 * 128)
    for copy in rest_copies:
        copy.start()

    square_e = (elems, elems)
    for j in range(4):
        seen = nbr[j:j + 1, :]
        key = jnp.where(seen < 4 * elems, seen & (elems - 1), -1)
        glb[j] = nn(ihl[...], ones_at(iota(square_e, 0) == key)).astype(BF)

    exchange_wait(2, qsend, qrecv, q_sem, loc_sem.at[0])
    eye_p = eye(128, 128)
    high, low = split(qrecv[...])
    asked = nt(eye_p, high) + nt(eye_p, low)
    slots = 2 * devices
    item = asked[AT_ITEM:AT_ITEM + 1].astype(jnp.int32) - 1
    oht[...] = ones_at(iota((4 * elems, slots), 0) == item)

    inside = (row > 0, row < n_row - 1, col > 0, col < n_col - 1)

    def unpack(copies, recv, pairs):
        for copy in copies:
            copy.wait_recv()
        for side in range(2):
            lanes = slice(side * 128, side * 128 + 128)
            for n, pair in enumerate(pairs):
                first = jnp.where(inside[2 * side], recv[2 * side, n], 0.0)
                second = jnp.where(inside[2 * side + 1], recv[2 * side + 1, n], 0.0)
                halves = [(pair[0], jnp.where(half, first, pltpu.roll(second, 64, 1)))]
                if pair[1] != pair[0]:
                    halves.append((pair[1], jnp.where(half, pltpu.roll(first, 64, 1), second)))
                for quant, value in halves:
                    high, low = split(padded(value))
                    block = Q_ORDER.index(quant) * 128
                    gtab[block:block + 64, lanes] = high
                    gtab[block + 64:block + 128, lanes] = low

    unpack(head_copies, hrecv, HEAD_PAIRS)

    def neighbours(j, start, stop):
        seen = nbr[j:j + 1, :]
        key = jnp.where(seen < 4 * elems, -1, seen & (elems - 1))
        code = 3 * (lax.shift_right_logical(seen, 8) & 3) + ocode[j:j + 1, :]
        got = nn(gtab[start:stop, :], ones_at(iota(square_e, 0) == key)).astype(BF) + glb[j, start:stop, :]
        for block in range(start // 128, stop // 128):
            at = block * 128 - start
            high, low = got[at:at + 64], got[at + 64:at + 128]
            turns = nn(w12[...], jnp.concatenate([high, high, low], axis=0))
            value = turns[0:24]
            for c in range(1, 12):
                value = jnp.where(code == c, turns[24 * c:24 * c + 24], value)
            nvals[j, Q_ORDER[block]] = value

    fvals[...] = jnp.zeros_like(fvals)
    for j in range(4):
        neighbours(j, 0, HEAD)
        lanes = slice(j * elems, (j + 1) * elems)
        x0, x3, x6 = (xs[q, 32 * j:32 * j + 24, :] for q in (0, 3, 6))
        n0, n3, n6 = (nvals[j, q] for q in (0, 3, 6))
        fvals[0:24, lanes] = 0.5 * (x3 + n3) + 0.5 * (x6 - n6)
        fvals[24:48, lanes] = 0.5 * (x0 + n0)

    high, low = split(fvals[...])
    held = nn(high, oht[...]) + nn(low, oht[...])
    slip = friction_solve(
        held[0:FACE],
        held[24:24 + FACE],
        asked[AT_SHEAR:AT_SHEAR + FACE],
        asked[AT_NORMAL:AT_NORMAL + FACE],
        asked[AT_STATE:AT_STATE + FACE],
        asked[AT_SLIP:AT_SLIP + FACE],
    )
    slip = jnp.concatenate([slip, jnp.zeros((64 - FACE, slots), F32)], axis=0)
    slip_high, slip_low = split(slip)
    going = jnp.zeros((devices, 128), F32)
    blank = jnp.zeros((64, slots), BF)
    for k in range(2):
        owner = ones_at(iota((devices, slots), 1) == 2 * iota((devices, slots), 0) + k)
        for part in (slip_high, slip_low):
            going = going + nt(owner, jnp.concatenate([part, blank] if k == 0 else [blank, part], axis=0))
    vsend[...] = going
    exchange_start(1, vsend, vrecv, v_sem, loc_sem.at[1])

    for group in GROUPS:
        for p in group:
            turned[p] = nn(wv[...], stacked_of(p))
            if p not in GROUPS[0]:
                xs[p] = nn(wp[...], stacked_of(p))
    for group in GROUPS:
        for p, total in star_block(turned, group):
            integ[p] = dofs[p * BASIS:(p + 1) * BASIS, :] + 0.25 * total

    def flux_block(j, side, first, read):
        totals = [None] * 3
        for q in range(QUANT):
            value = read(q)
            for i in range(3):
                r = ((j * 2 + side) * QUANT + first + i) * QUANT + q
                term = flux[r:r + 1, :] * value
                totals[i] = term if totals[i] is None else totals[i] + term
        return totals

    loads[2].wait()
    for j in range(4):
        for first in range(0, QUANT, 3):
            for i, total in enumerate(flux_block(j, 0, first, lambda q: xs[q, 32 * j:32 * j + 24, :])):
                comb[first + i, 24 * j:24 * j + 24, :] = total

    unpack(rest_copies, grecv, REST_PAIRS)
    for j in range(4):
        neighbours(j, HEAD, 9 * 128)
    for j in range(4):
        for first in range(0, QUANT, 3):
            for i, total in enumerate(flux_block(j, 1, first, lambda q: nvals[j, q])):
                spot = (first + i, slice(24 * j, 24 * j + 24))
                comb[spot[0], spot[1], :] = comb[spot[0], spot[1], :] + total

    pushed = nt(jnp.concatenate([slip_high[0:32], slip_low[0:32]], axis=0), oht[...])
    pushed = 2.0 * (pushed[0:24] + pushed[32:56])
    for j in range(4):
        spot = slice(24 * j, 24 * j + 24)
        part = pushed[:, j * elems:(j + 1) * elems]
        comb[3, spot, :] = comb[3, spot, :] - part
        comb[6, spot, :] = comb[6, spot, :] + part

    def lifted(value):
        high, low = split(value)
        return nn(wl[...], jnp.concatenate([high, high], axis=0)) + nn(wl[:, 0:96], low)

    for p in range(QUANT):
        result[p * BASIS:(p + 1) * BASIS, :] = integ[p] + 0.25 * lifted(comb[p])
    store = pltpu.make_async_copy(result, out, out_sem.at[0])
    store.start()

    exchange_wait(1, vsend, vrecv, v_sem, loc_sem.at[1])
    high, low = split(vrecv[...])
    both = ones_at(iota(square, 0) == part_row)
    own = nn(nt(eye_p, high).astype(BF), both) + nn(nt(eye_p, low).astype(BF), both)
    slip_out[...] = jnp.where(rank_row == 0, own[0:FACE], own[64:64 + FACE])

    store.wait()
    for copy in head_copies + rest_copies:
        copy.wait_send()
    exchange_end(2, qsend, q_sem)
    exchange_end(1, vsend, v_sem)


def solution(mesh):
    n_row, n_col = mesh.shape["row"], mesh.shape["col"]
    devices = n_row * n_col

    def per_device(dofs, star, flux, kxi, proj, lift, orient, nbr, ocode, slist, fpart, fitem, sh0, nm0, stv, slp):
        elems = dofs.shape[1]
        vmem, anywhere = pl.BlockSpec(memory_space=pltpu.VMEM), pl.BlockSpec(memory_space=pl.ANY)
        table = pltpu.VMEM((devices, 128), F32)
        pair = pltpu.SemaphoreType.DMA((2,))
        four = pltpu.SemaphoreType.DMA((4,))
        return pl.pallas_call(
            lambda *refs: kernel(n_row, n_col, *refs),
            out_shape=(
                jax.ShapeDtypeStruct(dofs.shape, F32),
                jax.ShapeDtypeStruct(slp.shape, F32),
            ),
            in_specs=[anywhere] * 3 + [vmem] * 13,
            out_specs=(anywhere, vmem),
            scratch_shapes=[
                pltpu.VMEM(dofs.shape, F32),
                pltpu.VMEM(star.shape, F32),
                pltpu.VMEM(flux.shape, F32),
                pltpu.VMEM(dofs.shape, F32),
                pltpu.VMEM((3 * BASIS, 192), BF),
                pltpu.VMEM((3 * BASIS, 192), BF),
                pltpu.VMEM((128, 192), BF),
                pltpu.VMEM((288, 192), F32),
                pltpu.VMEM((288, 192), BF),
                pltpu.VMEM((2, 4 * FACE, BASIS), F32),
                pltpu.VMEM((BASIS, 192), BF),
                pltpu.VMEM((2, QUANT, 3 * BASIS, elems), F32),
                pltpu.VMEM((QUANT, BASIS, elems), F32),
                pltpu.VMEM((QUANT * 128, elems), BF),
                pltpu.VMEM((QUANT, 128, elems), F32),
                pltpu.VMEM((4, QUANT * 128, elems), BF),
                pltpu.VMEM((QUANT * 128, elems), BF),
                pltpu.VMEM((4, QUANT, 24, elems), F32),
                pltpu.VMEM((QUANT, 96, elems), F32),
                pltpu.VMEM((64, 4 * elems), F32),
                pltpu.VMEM((4 * elems, 2 * devices), BF),
                pltpu.VMEM((128, 128), F32),
                pltpu.VMEM((4, 3, BASIS, 128), F32),
                pltpu.VMEM((4, 3, BASIS, 128), F32),
                pltpu.VMEM((4, 2, BASIS, 128), F32),
                pltpu.VMEM((4, 2, BASIS, 128), F32),
                pltpu.VMEM((2 * devices, 128), F32),
                pltpu.VMEM((2 * devices, 128), F32),
                table, table,
                four, four, four, four, pair, pair, pair,
                pltpu.SemaphoreType.DMA((3,)),
                pltpu.SemaphoreType.DMA((1,)),
            ],
            compiler_params=pltpu.CompilerParams(collective_id=0, has_side_effects=True),
        )(
            dofs, star, flux, kxi, jnp.transpose(proj, (2, 0, 1)), jnp.transpose(lift, (1, 0, 2)), orient,
            nbr, ocode, slist, fpart.reshape(1, -1), fitem.reshape(1, -1), sh0, nm0, stv, slp,
        )

    split_cols = P(None, ("row", "col"))
    placed = (
        (split_cols,) * 3
        + (P(),) * 4
        + (split_cols,) * 3
        + (P(("row", "col"), None), P(("row", "col")))
        + (split_cols,) * 4
    )
    return jax.shard_map(
        per_device, mesh=mesh, in_specs=placed, out_specs=(split_cols, split_cols), check_vma=False
    )
```

```python
import jax
import jax.numpy as jnp
from jax import lax
from jax.experimental import pallas as pl
from jax.experimental.pallas import tpu as pltpu
from jax.sharding import PartitionSpec as P

QUANT = 9
BASIS = 56
FACE = 21
ORDER = 6
NEWTON_ITERS = 3
TIME_STEP = 2.0
FRIC_A = 0.5
MESH = pl.DeviceIdType.MESH
LOGICAL = pl.DeviceIdType.LOGICAL
BF = jnp.bfloat16
F32 = jnp.float32

Q_ORDER = (0, 3, 6, 1, 2, 4, 5, 7, 8)
GROUPS = (Q_ORDER[0:3], Q_ORDER[3:6], Q_ORDER[6:9])
HEAD = 3 * 128
HEAD_PAIRS = ((0, 3), (6, 6))
REST_PAIRS = ((1, 2), (4, 5), (7, 8))
AT_SHEAR, AT_NORMAL, AT_STATE, AT_SLIP, AT_ITEM = 0, 24, 48, 72, 96


def iota(shape, dim):
    return lax.broadcasted_iota(jnp.int32, shape, dim)


def ones_at(mask):
    return jnp.where(mask, 1.0, 0.0).astype(BF)


def nn(a, b):
    return jnp.dot(a, b, preferred_element_type=F32)


def nt(a, b):
    return lax.dot_general(a, b, (((1,), (1,)), ((), ())), preferred_element_type=F32)


def split(x):
    high = x.astype(BF)
    return high, (x - high.astype(F32)).astype(BF)


def eye(rows, cols):
    return ones_at(iota((rows, cols), 0) == iota((rows, cols), 1))


def place(rows, cols, offsets):
    delta = iota((rows, cols), 1) - iota((rows, cols), 0)
    mask = delta == offsets[0]
    for offset in offsets[1:]:
        mask = mask | (delta == offset)
    return ones_at(mask)


def padded(x):
    return jnp.concatenate([x, jnp.zeros((8, x.shape[1]), F32)], axis=0)


def stacked(x):
    high, low = split(x)
    return jnp.concatenate([high, high, low], axis=0)


def inverse_sinh(value):
    magnitude = jnp.abs(value)
    squared = magnitude * magnitude
    positive = jnp.log1p(magnitude + squared / (1.0 + jnp.sqrt(1.0 + squared)))
    return jnp.where(value < 0.0, -positive, positive)


def friction_solve(shear, normal, shear_init, normal_init, state_var, slip_prev):
    shear_total = shear_init + shear
    normal_eff = normal_init * (1.0 + 0.5 * jnp.tanh(normal))
    growth = jnp.exp(state_var / FRIC_A) * 0.5
    slip_now = slip_prev
    for _ in range(NEWTON_ITERS):
        scaled = growth * slip_now
        misfit = shear_total - slip_now - FRIC_A * normal_eff * inverse_sinh(scaled)
        slope_val = -1.0 - FRIC_A * normal_eff * growth / jnp.sqrt(1.0 + scaled * scaled)
        slip_now = slip_now - misfit / slope_val
    return slip_now


def kernel(
    n_row, n_col,
    dofs_in, star_in, flux_in, kxi, proj, lift, orient, nbr, ocode, slist, fpart, fitem, sh0, nm0, stv, slp,
    out, slip_out,
    dofs, star, flux,
    wk, wv, wp, wo, w12, tall, wl, adv, integ, ihl, xs, glb, gtab, nvals, comb, fvals, oht, params,
    gsend, grecv, hsend, hrecv, qsend, qrecv, vsend, vrecv,
    gs_sem, gr_sem, hs_sem, hr_sem, q_sem, v_sem, loc_sem, in_sem,
):
    devices = n_row * n_col
    loads = [
        pltpu.make_async_copy(source, target, in_sem.at[n])
        for n, (source, target) in enumerate(((dofs_in, dofs), (star_in, star), (flux_in, flux)))
    ]
    for load in loads:
        load.start()
    row, col = lax.axis_index("row"), lax.axis_index("col")
    me = row * n_col + col

    barrier = pltpu.get_barrier_semaphore()

    def ring(at, size, scale):
        return [lax.rem(at + step, size) * scale for step in range(size)]

    across = ring(row, n_row, n_col)
    deep = ring(col // 8, 4, 8)
    wide = ring(lax.rem(col, 8) // 2, 4, 2)
    core = ring(lax.rem(col, 2), 2, 1)
    hops = (0, 1, 2, 1)
    steps = [(y, z, x, c) for y in range(4) for z in range(4) for x in range(4) for c in range(2)][1:]
    steps.sort(key=lambda at: -(hops[at[0]] + hops[at[1]] + hops[at[2]]))

    def partner(at):
        return (across[at[0]] + deep[at[1]]) + (wide[at[2]] + core[at[3]])

    for at in steps:
        pl.semaphore_signal(barrier, inc=1, device_id=partner(at), device_id_type=LOGICAL)

    def own_copy(n, send, recv, local_sem):
        mine = pl.ds(n * me, n)
        return pltpu.make_async_copy(send.at[mine], recv.at[mine], local_sem)

    def exchange_start(n, send, recv, sem, local_sem):
        for at in steps:
            p = partner(at)
            pltpu.make_async_remote_copy(
                src_ref=send.at[pl.ds(n * p, n)],
                dst_ref=recv.at[pl.ds(n * me, n)],
                send_sem=sem.at[0],
                recv_sem=sem.at[1],
                device_id=p,
                device_id_type=LOGICAL,
            ).start()
        own_copy(n, send, recv, local_sem).start()

    def exchange_wait(n, send, recv, sem, local_sem):
        part = pl.ds(0, n * (devices - 1))
        pltpu.make_async_copy(recv.at[part], recv.at[part], sem.at[1]).wait()
        own_copy(n, send, recv, local_sem).wait()

    def exchange_end(n, send, sem):
        part = pl.ds(0, n * (devices - 1))
        pltpu.make_async_copy(send.at[part], send.at[part], sem.at[0]).wait()

    at_high, at_low = place(BASIS, 192, (0, 128)), place(BASIS, 192, (64,))
    eye_b = eye(BASIS, BASIS)
    back, forth = [], []
    for d in range(3):
        high, low = split(kxi[d])
        forth.append(nn(high, at_high) + nn(low, at_low))
        back.append(nn(nt(eye_b, high).astype(BF), at_high) + nn(nt(eye_b, low).astype(BF), at_low))
    wk[...] = jnp.concatenate(back, axis=0).astype(BF)
    wv[...] = jnp.concatenate(forth, axis=0).astype(BF)
    square = (devices, fitem.shape[1])
    part_row = fpart[...]
    wide_part = jnp.sum(jnp.where(iota(square, 0) == iota(square, 1), part_row, 0), axis=1, keepdims=True)
    earlier = (wide_part == part_row) & (iota(square, 0) < iota(square, 1))
    rank_row = jnp.sum(jnp.where(earlier, 1, 0), axis=0, keepdims=True)
    tall_square = (2 * devices, fitem.shape[1])
    slot_of = ones_at(iota(tall_square, 0) == 2 * part_row + rank_row)
    params[...] = jnp.zeros_like(params)
    for at, table in ((AT_SHEAR, sh0), (AT_NORMAL, nm0), (AT_STATE, stv), (AT_SLIP, slp)):
        params[at:at + FACE, :] = table[...]
    params[AT_ITEM:AT_ITEM + 1, :] = (fitem[...] + 1).astype(F32)
    high, low = split(params[...])
    qsend[...] = nt(slot_of, high) + nt(slot_of, low)

    def put(weights, value, target, q):
        target[q] = nn(weights[...], stacked(padded(value)))

    loads[0].wait()
    loads[1].wait()
    for q in Q_ORDER:
        start = dofs[q * BASIS:(q + 1) * BASIS, :]
        integ[q] = TIME_STEP * start
        put(wk, start, adv.at[0], q)

    def star_block(source, group):
        sides = []
        for lanes in (slice(0, 128), slice(128, 256)):
            totals = [None] * 3
            for q in Q_ORDER:
                for d in range(3):
                    value = source[q, d * BASIS:(d + 1) * BASIS, lanes]
                    for i, p in enumerate(group):
                        r = (d * QUANT + p) * QUANT + q
                        term = star[r:r + 1, lanes] * value
                        totals[i] = term if totals[i] is None else totals[i] + term
            sides.append(totals)
        return [(p, jnp.concatenate([left, right], axis=1)) for p, left, right in zip(group, *sides)]

    factor = TIME_STEP
    for k in range(1, ORDER - 1):
        if k == 3:
            pl.semaphore_wait(barrier, devices - 1)
            exchange_start(2, qsend, qrecv, q_sem, loc_sem.at[0])
        factor = factor * TIME_STEP / (k + 1)
        source, target = adv.at[(k - 1) % 2], adv.at[k % 2]
        for group in GROUPS:
            for p, total in star_block(source, group):
                integ[p] = integ[p] + factor * total
                put(wk, total, target, p)
    factor = factor * TIME_STEP / ORDER
    source, turned = adv.at[(ORDER - 2) % 2], adv.at[(ORDER - 1) % 2]

    small = slist.shape[1]
    elems = dofs.shape[1]
    spread = ones_at(lax.rem(iota((small, 4 * small), 1), small) == iota((small, 4 * small), 0))
    listed = nn(slist[...].astype(F32).astype(BF), spread)
    listed = jnp.sum(
        jnp.where(iota((4, 4 * small), 1) // small == iota((4, 4 * small), 0), listed, 0.0), axis=0, keepdims=True
    ).astype(jnp.int32)
    half = iota((BASIS, 128), 1) < 64
    targets = (
        lax.rem(row + 1, n_row) * n_col + col,
        lax.rem(row + n_row - 1, n_row) * n_col + col,
        row * n_col + lax.rem(col + 1, n_col),
        row * n_col + lax.rem(col + n_col - 1, n_col),
    )

    def ghost_copies(send, recv, send_sem, recv_sem):
        return [
            pltpu.make_async_remote_copy(
                src_ref=send.at[d],
                dst_ref=recv.at[d],
                send_sem=send_sem.at[d],
                recv_sem=recv_sem.at[d],
                device_id=targets[d],
                device_id_type=LOGICAL,
            )
            for d in range(4)
        ]

    head_copies = ghost_copies(hsend, hrecv, hs_sem, hr_sem)
    rest_copies = ghost_copies(gsend, grecv, gs_sem, gr_sem)

    def pack(send, pairs, start, stop):
        picked = nn(ihl[start:stop, :], ones_at(iota((elems, 4 * small), 0) == listed))
        for side in range(2):
            lanes = slice(side * 128, side * 128 + 128)
            for n, pair in enumerate(pairs):
                ends = []
                for q in pair:
                    at = Q_ORDER.index(q) * 128 - start
                    ends.append(picked[at:at + BASIS, lanes] + picked[at + 64:at + 64 + BASIS, lanes])
                first, second = ends
                send[2 * side, n] = jnp.where(half, first, pltpu.roll(second, 64, 1))
                send[2 * side + 1, n] = jnp.where(half, pltpu.roll(first, 64, 1), second)

    def finish(group):
        for p, total in star_block(source, group):
            high, low = split(padded(integ[p] + factor * total))
            block = Q_ORDER.index(p) * 128
            ihl[block:block + 64, :] = high
            ihl[block + 64:block + 128, :] = low

    def stacked_of(p):
        block = Q_ORDER.index(p) * 128
        high = ihl[block:block + 64, :]
        return jnp.concatenate([high, high, ihl[block + 64:block + 128, :]], axis=0)

    finish(GROUPS[0])
    pack(hsend, HEAD_PAIRS, 0, HEAD)
    for copy in head_copies:
        copy.start()

    flat = 4 * FACE
    for g in range(FACE):
        tall[0, 4 * g:4 * g + 4, :] = proj[g]
        tall[1, 4 * g:4 * g + 4, :] = lift[g]
    shape = (128, flat)
    order = ones_at((iota(shape, 0) // 32 + 4 * lax.rem(iota(shape, 0), 32)) == iota(shape, 1))
    high, low = split(tall[0])
    proj_high, proj_low = nn(order, high).astype(BF), nn(order, low).astype(BF)
    wp[...] = (nn(proj_high, at_high) + nn(proj_low, at_low)).astype(BF)
    rows = []
    pick_g = eye(24, FACE)
    turn_high, turn_low = place(FACE, 96, (0, 64)), place(FACE, 96, (32,))
    for o in range(3):
        high, low = split(orient[o])
        rows.append(nn(nt(pick_g, high).astype(BF), turn_high) + nn(nt(pick_g, low).astype(BF), turn_low))
    turn = jnp.concatenate(rows, axis=0).astype(BF)
    for j in range(4):
        own_rows = slice(32 * j, 32 * j + 32)
        both = jnp.concatenate([proj_high[own_rows], proj_high[own_rows], proj_low[own_rows]], axis=0)
        high, low = split(nn(turn, both))
        wo[72 * j:72 * j + 72, :] = nn(high, at_high) + nn(low, at_low)
    w12[...] = wo[...].astype(BF)
    for p in GROUPS[0]:
        xs[p] = nn(wp[...], stacked_of(p))
    finish(GROUPS[1])
    finish(GROUPS[2])
    pack(gsend, REST_PAIRS, HEAD, 9 * 128)
    for copy in rest_copies:
        copy.start()

    square_e = (elems, elems)
    for j in range(4):
        seen = nbr[j:j + 1, :]
        key = jnp.where(seen < 4 * elems, seen & (elems - 1), -1)
        glb[j] = nn(ihl[...], ones_at(iota(square_e, 0) == key)).astype(BF)

    exchange_wait(2, qsend, qrecv, q_sem, loc_sem.at[0])
    eye_p = eye(128, 128)
    high, low = split(qrecv[...])
    asked = nt(eye_p, high) + nt(eye_p, low)
    slots = 2 * devices
    item = asked[AT_ITEM:AT_ITEM + 1].astype(jnp.int32) - 1
    oht[...] = ones_at(iota((4 * elems, slots), 0) == item)

    inside = (row > 0, row < n_row - 1, col > 0, col < n_col - 1)

    def unpack(copies, recv, pairs):
        for copy in copies:
            copy.wait_recv()
        for side in range(2):
            lanes = slice(side * 128, side * 128 + 128)
            for n, pair in enumerate(pairs):
                first = jnp.where(inside[2 * side], recv[2 * side, n], 0.0)
                second = jnp.where(inside[2 * side + 1], recv[2 * side + 1, n], 0.0)
                halves = [(pair[0], jnp.where(half, first, pltpu.roll(second, 64, 1)))]
                if pair[1] != pair[0]:
                    halves.append((pair[1], jnp.where(half, pltpu.roll(first, 64, 1), second)))
                for quant, value in halves:
                    high, low = split(padded(value))
                    block = Q_ORDER.index(quant) * 128
                    gtab[block:block + 64, lanes] = high
                    gtab[block + 64:block + 128, lanes] = low

    unpack(head_copies, hrecv, HEAD_PAIRS)

    def neighbours(j, start, stop):
        seen = nbr[j:j + 1, :]
        key = jnp.where(seen < 4 * elems, -1, seen & (elems - 1))
        code = 3 * (lax.shift_right_logical(seen, 8) & 3) + ocode[j:j + 1, :]
        got = nn(gtab[start:stop, :], ones_at(iota(square_e, 0) == key)).astype(BF) + glb[j, start:stop, :]
        for block in range(start // 128, stop // 128):
            at = block * 128 - start
            high, low = got[at:at + 64], got[at + 64:at + 128]
            turns = nn(w12[...], jnp.concatenate([high, high, low], axis=0))
            value = turns[0:24]
            for c in range(1, 12):
                value = jnp.where(code == c, turns[24 * c:24 * c + 24], value)
            nvals[j, Q_ORDER[block]] = value

    fvals[...] = jnp.zeros_like(fvals)
    for j in range(4):
        neighbours(j, 0, HEAD)
        lanes = slice(j * elems, (j + 1) * elems)
        x0, x3, x6 = (xs[q, 32 * j:32 * j + 24, :] for q in (0, 3, 6))
        n0, n3, n6 = (nvals[j, q] for q in (0, 3, 6))
        fvals[0:24, lanes] = 0.5 * (x3 + n3) + 0.5 * (x6 - n6)
        fvals[24:48, lanes] = 0.5 * (x0 + n0)

    high, low = split(fvals[...])
    held = nn(high, oht[...]) + nn(low, oht[...])
    slip = friction_solve(
        held[0:FACE],
        held[24:24 + FACE],
        asked[AT_SHEAR:AT_SHEAR + FACE],
        asked[AT_NORMAL:AT_NORMAL + FACE],
        asked[AT_STATE:AT_STATE + FACE],
        asked[AT_SLIP:AT_SLIP + FACE],
    )
    slip = jnp.concatenate([slip, jnp.zeros((64 - FACE, slots), F32)], axis=0)
    slip_high, slip_low = split(slip)
    going = jnp.zeros((devices, 128), F32)
    blank = jnp.zeros((64, slots), BF)
    for k in range(2):
        owner = ones_at(iota((devices, slots), 1) == 2 * iota((devices, slots), 0) + k)
        for part in (slip_high, slip_low):
            going = going + nt(owner, jnp.concatenate([part, blank] if k == 0 else [blank, part], axis=0))
    vsend[...] = going
    exchange_start(1, vsend, vrecv, v_sem, loc_sem.at[1])

    shape = (flat, 192)
    spot = 24 * lax.rem(iota(shape, 0), 4) + iota(shape, 0) // 4
    high, low = split(tall[1])
    table = nn(nt(eye_b, high).astype(BF), ones_at(iota(shape, 1) == spot))
    table = table + nn(nt(eye_b, low).astype(BF), ones_at(iota(shape, 1) == spot + 96))
    wl[...] = table.astype(BF)

    for group in GROUPS:
        for p in group:
            turned[p] = nn(wv[...], stacked_of(p))
            if p not in GROUPS[0]:
                xs[p] = nn(wp[...], stacked_of(p))
    for group in GROUPS:
        for p, total in star_block(turned, group):
            integ[p] = dofs[p * BASIS:(p + 1) * BASIS, :] + 0.25 * total

    def flux_block(j, side, first, read):
        totals = [None] * 3
        for q in range(QUANT):
            value = read(q)
            for i in range(3):
                r = ((j * 2 + side) * QUANT + first + i) * QUANT + q
                term = flux[r:r + 1, :] * value
                totals[i] = term if totals[i] is None else totals[i] + term
        return totals

    loads[2].wait()
    for j in range(4):
        for first in range(0, QUANT, 3):
            for i, total in enumerate(flux_block(j, 0, first, lambda q: xs[q, 32 * j:32 * j + 24, :])):
                comb[first + i, 24 * j:24 * j + 24, :] = total

    unpack(rest_copies, grecv, REST_PAIRS)
    for j in range(4):
        neighbours(j, HEAD, 9 * 128)
    for j in range(4):
        for first in range(0, QUANT, 3):
            for i, total in enumerate(flux_block(j, 1, first, lambda q: nvals[j, q])):
                spot = (first + i, slice(24 * j, 24 * j + 24))
                comb[spot[0], spot[1], :] = comb[spot[0], spot[1], :] + total

    pushed = nt(jnp.concatenate([slip_high[0:32], slip_low[0:32]], axis=0), oht[...])
    pushed = 2.0 * (pushed[0:24] + pushed[32:56])
    for j in range(4):
        spot = slice(24 * j, 24 * j + 24)
        part = pushed[:, j * elems:(j + 1) * elems]
        comb[3, spot, :] = comb[3, spot, :] - part
        comb[6, spot, :] = comb[6, spot, :] + part

    def lifted(value):
        high, low = split(value)
        return nn(wl[...], jnp.concatenate([high, high], axis=0)) + nn(wl[:, 0:96], low)

    for p in range(QUANT):
        out[p * BASIS:(p + 1) * BASIS, :] = integ[p] + 0.25 * lifted(comb[p])

    exchange_wait(1, vsend, vrecv, v_sem, loc_sem.at[1])
    high, low = split(vrecv[...])
    both = ones_at(iota(square, 0) == part_row)
    own = nn(nt(eye_p, high).astype(BF), both) + nn(nt(eye_p, low).astype(BF), both)
    slip_out[...] = jnp.where(rank_row == 0, own[0:FACE], own[64:64 + FACE])

    for copy in head_copies + rest_copies:
        copy.wait_send()
    exchange_end(2, qsend, q_sem)
    exchange_end(1, vsend, v_sem)


def store_results(dofs_ref, slip_ref, dofs_out, slip_out, sem):
    copies = [
        pltpu.make_async_copy(source, target, sem.at[n])
        for n, (source, target) in enumerate(((dofs_ref, dofs_out), (slip_ref, slip_out)))
    ]
    for copy in copies:
        copy.start()
    for copy in copies:
        copy.wait()


def solution(mesh):
    n_row, n_col = mesh.shape["row"], mesh.shape["col"]
    devices = n_row * n_col

    def per_device(dofs, star, flux, kxi, proj, lift, orient, nbr, ocode, slist, fpart, fitem, sh0, nm0, stv, slp):
        elems = dofs.shape[1]
        vmem, anywhere = pl.BlockSpec(memory_space=pltpu.VMEM), pl.BlockSpec(memory_space=pl.ANY)
        table = pltpu.VMEM((devices, 128), F32)
        pair = pltpu.SemaphoreType.DMA((2,))
        four = pltpu.SemaphoreType.DMA((4,))
        inside = pl.pallas_call(
            lambda *refs: kernel(n_row, n_col, *refs),
            out_shape=(pltpu.VMEM(dofs.shape, F32), pltpu.VMEM(slp.shape, F32)),
            in_specs=[anywhere] * 3 + [vmem] * 13,
            out_specs=(vmem, vmem),
            scratch_shapes=[
                pltpu.VMEM(dofs.shape, F32),
                pltpu.VMEM(star.shape, F32),
                pltpu.VMEM(flux.shape, F32),
                pltpu.VMEM((3 * BASIS, 192), BF),
                pltpu.VMEM((3 * BASIS, 192), BF),
                pltpu.VMEM((128, 192), BF),
                pltpu.VMEM((288, 192), F32),
                pltpu.VMEM((288, 192), BF),
                pltpu.VMEM((2, 4 * FACE, BASIS), F32),
                pltpu.VMEM((BASIS, 192), BF),
                pltpu.VMEM((2, QUANT, 3 * BASIS, elems), F32),
                pltpu.VMEM((QUANT, BASIS, elems), F32),
                pltpu.VMEM((QUANT * 128, elems), BF),
                pltpu.VMEM((QUANT, 128, elems), F32),
                pltpu.VMEM((4, QUANT * 128, elems), BF),
                pltpu.VMEM((QUANT * 128, elems), BF),
                pltpu.VMEM((4, QUANT, 24, elems), F32),
                pltpu.VMEM((QUANT, 96, elems), F32),
                pltpu.VMEM((64, 4 * elems), F32),
                pltpu.VMEM((4 * elems, 2 * devices), BF),
                pltpu.VMEM((128, 128), F32),
                pltpu.VMEM((4, 3, BASIS, 128), F32),
                pltpu.VMEM((4, 3, BASIS, 128), F32),
                pltpu.VMEM((4, 2, BASIS, 128), F32),
                pltpu.VMEM((4, 2, BASIS, 128), F32),
                pltpu.VMEM((2 * devices, 128), F32),
                pltpu.VMEM((2 * devices, 128), F32),
                table, table,
                four, four, four, four, pair, pair, pair,
                pltpu.SemaphoreType.DMA((3,)),
            ],
            compiler_params=pltpu.CompilerParams(collective_id=0, has_side_effects=True),
        )(
            dofs, star, flux, kxi, jnp.transpose(proj, (2, 0, 1)), jnp.transpose(lift, (1, 0, 2)), orient,
            nbr, ocode, slist, fpart.reshape(1, -1), fitem.reshape(1, -1), sh0, nm0, stv, slp,
        )
        return pl.pallas_call(
            store_results,
            out_shape=(jax.ShapeDtypeStruct(dofs.shape, F32), jax.ShapeDtypeStruct(slp.shape, F32)),
            in_specs=[vmem] * 2,
            out_specs=(anywhere, anywhere),
            scratch_shapes=[pair],
            compiler_params=pltpu.CompilerParams(vmem_limit_bytes=1024 * 1024),
        )(*inside)

    split_cols = P(None, ("row", "col"))
    placed = (
        (split_cols,) * 3
        + (P(),) * 4
        + (split_cols,) * 3
        + (P(("row", "col"), None), P(("row", "col")))
        + (split_cols,) * 4
    )
    return jax.shard_map(
        per_device, mesh=mesh, in_specs=placed, out_specs=(split_cols, split_cols), check_vma=False
    )
```

```python
import jax
import jax.numpy as jnp
from jax import lax
from jax.experimental import pallas as pl
from jax.experimental.pallas import tpu as pltpu
from jax.sharding import PartitionSpec as P

QUANT = 9
BASIS = 56
FACE = 21
ORDER = 6
NEWTON_ITERS = 3
TIME_STEP = 2.0
FRIC_A = 0.5
MESH = pl.DeviceIdType.MESH
LOGICAL = pl.DeviceIdType.LOGICAL
BF = jnp.bfloat16
F32 = jnp.float32

DIFF = 9
BLOCKS = (0, DIFF, 3, 1, 2, 4, 5, 7, 8, 6)
GROUPS = ((0, 3, 6), (1, 2, 4), (5, 7, 8))
HEAD, ALL = 2 * 128, 9 * 128
HEAD_PAIRS = ((0, DIFF),)
REST_PAIRS = ((3, 1), (2, 4), (5, 7), (8, 8))
AT_SHEAR, AT_NORMAL, AT_STATE, AT_SLIP, AT_ITEM = 0, 24, 48, 72, 96


def iota(shape, dim):
    return lax.broadcasted_iota(jnp.int32, shape, dim)


def ones_at(mask):
    return jnp.where(mask, 1.0, 0.0).astype(BF)


def nn(a, b):
    return jnp.dot(a, b, preferred_element_type=F32)


def nt(a, b):
    return lax.dot_general(a, b, (((1,), (1,)), ((), ())), preferred_element_type=F32)


def split(x):
    high = x.astype(BF)
    return high, (x - high.astype(F32)).astype(BF)


def eye(rows, cols):
    return ones_at(iota((rows, cols), 0) == iota((rows, cols), 1))


def place(rows, cols, offsets):
    delta = iota((rows, cols), 1) - iota((rows, cols), 0)
    mask = delta == offsets[0]
    for offset in offsets[1:]:
        mask = mask | (delta == offset)
    return ones_at(mask)


def padded(x):
    return jnp.concatenate([x, jnp.zeros((8, x.shape[1]), F32)], axis=0)


def stacked(x):
    high, low = split(x)
    return jnp.concatenate([high, high, low], axis=0)


def inverse_sinh(value):
    magnitude = jnp.abs(value)
    squared = magnitude * magnitude
    positive = jnp.log1p(magnitude + squared / (1.0 + jnp.sqrt(1.0 + squared)))
    return jnp.where(value < 0.0, -positive, positive)


def friction_solve(shear, normal, shear_init, normal_init, state_var, slip_prev):
    shear_total = shear_init + shear
    normal_eff = normal_init * (1.0 + 0.5 * jnp.tanh(normal))
    growth = jnp.exp(state_var / FRIC_A) * 0.5
    slip_now = slip_prev
    for _ in range(NEWTON_ITERS):
        scaled = growth * slip_now
        misfit = shear_total - slip_now - FRIC_A * normal_eff * inverse_sinh(scaled)
        slope_val = -1.0 - FRIC_A * normal_eff * growth / jnp.sqrt(1.0 + scaled * scaled)
        slip_now = slip_now - misfit / slope_val
    return slip_now


def kernel(
    n_row, n_col,
    dofs_in, star_in, flux_in, kxi, proj, lift, orient, nbr, ocode, slist, fpart, fitem, sh0, nm0, stv, slp,
    out, slip_out,
    dofs, star, flux,
    wk, wv, wp, wo, w12, tall, wl, adv, integ, ihl, xs, glb, gtab, nvals, comb, fvals, oht, params,
    gsend, grecv, hsend, hrecv, qsend, qrecv, vsend, vrecv,
    gs_sem, gr_sem, hs_sem, hr_sem, q_sem, v_sem, loc_sem, in_sem,
):
    devices = n_row * n_col
    loads = [
        pltpu.make_async_copy(source, target, in_sem.at[n])
        for n, (source, target) in enumerate(((dofs_in, dofs), (star_in, star), (flux_in, flux)))
    ]
    for load in loads:
        load.start()
    row, col = lax.axis_index("row"), lax.axis_index("col")
    me = row * n_col + col

    barrier = pltpu.get_barrier_semaphore()

    def ring(at, size, scale):
        return [lax.rem(at + step, size) * scale for step in range(size)]

    across = ring(row, n_row, n_col)
    deep = ring(col // 8, 4, 8)
    wide = ring(lax.rem(col, 8) // 2, 4, 2)
    core = ring(lax.rem(col, 2), 2, 1)
    hops = (0, 1, 2, 1)
    steps = [(y, z, x, c) for y in range(4) for z in range(4) for x in range(4) for c in range(2)][1:]
    steps.sort(key=lambda at: -(hops[at[0]] + hops[at[1]] + hops[at[2]]))

    def partner(at):
        return (across[at[0]] + deep[at[1]]) + (wide[at[2]] + core[at[3]])

    for at in steps:
        pl.semaphore_signal(barrier, inc=1, device_id=partner(at), device_id_type=LOGICAL)

    def own_copy(n, send, recv, local_sem):
        mine = pl.ds(n * me, n)
        return pltpu.make_async_copy(send.at[mine], recv.at[mine], local_sem)

    def exchange_start(n, send, recv, sem, local_sem):
        for at in steps:
            p = partner(at)
            pltpu.make_async_remote_copy(
                src_ref=send.at[pl.ds(n * p, n)],
                dst_ref=recv.at[pl.ds(n * me, n)],
                send_sem=sem.at[0],
                recv_sem=sem.at[1],
                device_id=p,
                device_id_type=LOGICAL,
            ).start()
        own_copy(n, send, recv, local_sem).start()

    def exchange_wait(n, send, recv, sem, local_sem):
        part = pl.ds(0, n * (devices - 1))
        pltpu.make_async_copy(recv.at[part], recv.at[part], sem.at[1]).wait()
        own_copy(n, send, recv, local_sem).wait()

    def exchange_end(n, send, sem):
        part = pl.ds(0, n * (devices - 1))
        pltpu.make_async_copy(send.at[part], send.at[part], sem.at[0]).wait()

    at_high, at_low = place(BASIS, 192, (0, 128)), place(BASIS, 192, (64,))
    eye_b = eye(BASIS, BASIS)
    back, forth = [], []
    for d in range(3):
        high, low = split(kxi[d])
        forth.append(nn(high, at_high) + nn(low, at_low))
        back.append(nn(nt(eye_b, high).astype(BF), at_high) + nn(nt(eye_b, low).astype(BF), at_low))
    wk[...] = jnp.concatenate(back, axis=0).astype(BF)
    wv[...] = jnp.concatenate(forth, axis=0).astype(BF)
    square = (devices, fitem.shape[1])
    part_row = fpart[...]
    wide_part = jnp.sum(jnp.where(iota(square, 0) == iota(square, 1), part_row, 0), axis=1, keepdims=True)
    earlier = (wide_part == part_row) & (iota(square, 0) < iota(square, 1))
    rank_row = jnp.sum(jnp.where(earlier, 1, 0), axis=0, keepdims=True)
    tall_square = (2 * devices, fitem.shape[1])
    slot_of = ones_at(iota(tall_square, 0) == 2 * part_row + rank_row)
    params[...] = jnp.zeros_like(params)
    for at, table in ((AT_SHEAR, sh0), (AT_NORMAL, nm0), (AT_STATE, stv), (AT_SLIP, slp)):
        params[at:at + FACE, :] = table[...]
    params[AT_ITEM:AT_ITEM + 1, :] = (fitem[...] + 1).astype(F32)
    high, low = split(params[...])
    qsend[...] = nt(slot_of, high) + nt(slot_of, low)

    def put(weights, value, target, q):
        target[q] = nn(weights[...], stacked(padded(value)))

    loads[0].wait()
    loads[1].wait()
    for q in (0, 3, 6, 1, 2, 4, 5, 7, 8):
        start = dofs[q * BASIS:(q + 1) * BASIS, :]
        integ[q] = TIME_STEP * start
        put(wk, start, adv.at[0], q)

    def star_block(source, group):
        sides = []
        for lanes in (slice(0, 128), slice(128, 256)):
            totals = [None] * 3
            for q in (0, 3, 6, 1, 2, 4, 5, 7, 8):
                for d in range(3):
                    value = source[q, d * BASIS:(d + 1) * BASIS, lanes]
                    for i, p in enumerate(group):
                        r = (d * QUANT + p) * QUANT + q
                        term = star[r:r + 1, lanes] * value
                        totals[i] = term if totals[i] is None else totals[i] + term
            sides.append(totals)
        return [(p, jnp.concatenate([left, right], axis=1)) for p, left, right in zip(group, *sides)]

    factor = TIME_STEP
    for k in range(1, ORDER - 1):
        if k == 3:
            pl.semaphore_wait(barrier, devices - 1)
            exchange_start(2, qsend, qrecv, q_sem, loc_sem.at[0])
        factor = factor * TIME_STEP / (k + 1)
        source, target = adv.at[(k - 1) % 2], adv.at[k % 2]
        for group in GROUPS:
            for p, total in star_block(source, group):
                integ[p] = integ[p] + factor * total
                put(wk, total, target, p)
    factor = factor * TIME_STEP / ORDER
    source, turned = adv.at[(ORDER - 2) % 2], adv.at[(ORDER - 1) % 2]

    small = slist.shape[1]
    elems = dofs.shape[1]
    spread = ones_at(lax.rem(iota((small, 4 * small), 1), small) == iota((small, 4 * small), 0))
    listed = nn(slist[...].astype(F32).astype(BF), spread)
    listed = jnp.sum(
        jnp.where(iota((4, 4 * small), 1) // small == iota((4, 4 * small), 0), listed, 0.0), axis=0, keepdims=True
    ).astype(jnp.int32)
    half = iota((BASIS, 128), 1) < 64
    targets = (
        lax.rem(row + 1, n_row) * n_col + col,
        lax.rem(row + n_row - 1, n_row) * n_col + col,
        row * n_col + lax.rem(col + 1, n_col),
        row * n_col + lax.rem(col + n_col - 1, n_col),
    )

    def ghost_copies(send, recv, send_sem, recv_sem):
        return [
            pltpu.make_async_remote_copy(
                src_ref=send.at[d],
                dst_ref=recv.at[d],
                send_sem=send_sem.at[d],
                recv_sem=recv_sem.at[d],
                device_id=targets[d],
                device_id_type=LOGICAL,
            )
            for d in range(4)
        ]

    head_copies = ghost_copies(hsend, hrecv, hs_sem, hr_sem)
    rest_copies = ghost_copies(gsend, grecv, gs_sem, gr_sem)

    def pack(send, pairs, start, stop):
        picked = nn(ihl[start:stop, :], ones_at(iota((elems, 4 * small), 0) == listed))
        for side in range(2):
            lanes = slice(side * 128, side * 128 + 128)
            for n, pair in enumerate(pairs):
                ends = []
                for q in pair:
                    at = BLOCKS.index(q) * 128 - start
                    ends.append(picked[at:at + BASIS, lanes] + picked[at + 64:at + 64 + BASIS, lanes])
                first, second = ends
                send[2 * side, n] = jnp.where(half, first, pltpu.roll(second, 64, 1))
                send[2 * side + 1, n] = jnp.where(half, pltpu.roll(first, 64, 1), second)

    def finish(group):
        values = {p: integ[p] + factor * total for p, total in star_block(source, group)}
        if group == GROUPS[0]:
            values[DIFF] = values[3] - values[6]
        for p, value in values.items():
            high, low = split(padded(value))
            block = BLOCKS.index(p) * 128
            ihl[block:block + 64, :] = high
            ihl[block + 64:block + 128, :] = low

    def stacked_of(p):
        block = BLOCKS.index(p) * 128
        high = ihl[block:block + 64, :]
        return jnp.concatenate([high, high, ihl[block + 64:block + 128, :]], axis=0)

    finish(GROUPS[0])
    pack(hsend, HEAD_PAIRS, 0, HEAD)
    for copy in head_copies:
        copy.start()

    flat = 4 * FACE
    for g in range(FACE):
        tall[0, 4 * g:4 * g + 4, :] = proj[g]
        tall[1, 4 * g:4 * g + 4, :] = lift[g]
    shape = (128, flat)
    order = ones_at((iota(shape, 0) // 32 + 4 * lax.rem(iota(shape, 0), 32)) == iota(shape, 1))
    high, low = split(tall[0])
    proj_high, proj_low = nn(order, high).astype(BF), nn(order, low).astype(BF)
    wp[...] = (nn(proj_high, at_high) + nn(proj_low, at_low)).astype(BF)
    rows = []
    pick_g = eye(24, FACE)
    turn_high, turn_low = place(FACE, 96, (0, 64)), place(FACE, 96, (32,))
    for o in range(3):
        high, low = split(orient[o])
        rows.append(nn(nt(pick_g, high).astype(BF), turn_high) + nn(nt(pick_g, low).astype(BF), turn_low))
    turn = jnp.concatenate(rows, axis=0).astype(BF)
    for j in range(4):
        own_rows = slice(32 * j, 32 * j + 32)
        both = jnp.concatenate([proj_high[own_rows], proj_high[own_rows], proj_low[own_rows]], axis=0)
        high, low = split(nn(turn, both))
        wo[72 * j:72 * j + 72, :] = nn(high, at_high) + nn(low, at_low)
    w12[...] = wo[...].astype(BF)
    for p in GROUPS[0]:
        xs[p] = nn(wp[...], stacked_of(p))
    finish(GROUPS[1])
    finish(GROUPS[2])
    pack(gsend, REST_PAIRS, HEAD, ALL)
    for copy in rest_copies:
        copy.start()

    square_e = (elems, elems)
    for j in range(4):
        seen = nbr[j:j + 1, :]
        key = jnp.where(seen < 4 * elems, seen & (elems - 1), -1)
        glb[j] = nn(ihl[0:ALL, :], ones_at(iota(square_e, 0) == key)).astype(BF)

    exchange_wait(2, qsend, qrecv, q_sem, loc_sem.at[0])
    eye_p = eye(128, 128)
    high, low = split(qrecv[...])
    asked = nt(eye_p, high) + nt(eye_p, low)
    slots = 2 * devices
    item = asked[AT_ITEM:AT_ITEM + 1].astype(jnp.int32) - 1
    oht[...] = ones_at(iota((4 * elems, slots), 0) == item)

    inside = (row > 0, row < n_row - 1, col > 0, col < n_col - 1)

    def unpack(copies, recv, pairs):
        for copy in copies:
            copy.wait_recv()
        for side in range(2):
            lanes = slice(side * 128, side * 128 + 128)
            for n, pair in enumerate(pairs):
                first = jnp.where(inside[2 * side], recv[2 * side, n], 0.0)
                second = jnp.where(inside[2 * side + 1], recv[2 * side + 1, n], 0.0)
                halves = [(pair[0], jnp.where(half, first, pltpu.roll(second, 64, 1)))]
                if pair[1] != pair[0]:
                    halves.append((pair[1], jnp.where(half, pltpu.roll(first, 64, 1), second)))
                for quant, value in halves:
                    high, low = split(padded(value))
                    block = BLOCKS.index(quant) * 128
                    gtab[block:block + 64, lanes] = high
                    gtab[block + 64:block + 128, lanes] = low

    unpack(head_copies, hrecv, HEAD_PAIRS)

    def neighbours(j, start, stop):
        seen = nbr[j:j + 1, :]
        key = jnp.where(seen < 4 * elems, -1, seen & (elems - 1))
        code = 3 * (lax.shift_right_logical(seen, 8) & 3) + ocode[j:j + 1, :]
        got = nn(gtab[start:stop, :], ones_at(iota(square_e, 0) == key)).astype(BF) + glb[j, start:stop, :]
        for block in range(start // 128, stop // 128):
            at = block * 128 - start
            high, low = got[at:at + 64], got[at + 64:at + 128]
            turns = nn(w12[...], jnp.concatenate([high, high, low], axis=0))
            value = turns[0:24]
            for c in range(1, 12):
                value = jnp.where(code == c, turns[24 * c:24 * c + 24], value)
            nvals[j, BLOCKS[block]] = value

    fvals[...] = jnp.zeros_like(fvals)
    for j in range(4):
        neighbours(j, 0, HEAD)
        lanes = slice(j * elems, (j + 1) * elems)
        x0, x3, x6 = (xs[q, 32 * j:32 * j + 24, :] for q in (0, 3, 6))
        fvals[0:24, lanes] = 0.5 * (x3 + x6) + 0.5 * nvals[j, DIFF]
        fvals[24:48, lanes] = 0.5 * (x0 + nvals[j, 0])

    high, low = split(fvals[...])
    held = nn(high, oht[...]) + nn(low, oht[...])
    slip = friction_solve(
        held[0:FACE],
        held[24:24 + FACE],
        asked[AT_SHEAR:AT_SHEAR + FACE],
        asked[AT_NORMAL:AT_NORMAL + FACE],
        asked[AT_STATE:AT_STATE + FACE],
        asked[AT_SLIP:AT_SLIP + FACE],
    )
    slip = jnp.concatenate([slip, jnp.zeros((64 - FACE, slots), F32)], axis=0)
    slip_high, slip_low = split(slip)
    going = jnp.zeros((devices, 128), F32)
    blank = jnp.zeros((64, slots), BF)
    for k in range(2):
        owner = ones_at(iota((devices, slots), 1) == 2 * iota((devices, slots), 0) + k)
        for part in (slip_high, slip_low):
            going = going + nt(owner, jnp.concatenate([part, blank] if k == 0 else [blank, part], axis=0))
    vsend[...] = going
    exchange_start(1, vsend, vrecv, v_sem, loc_sem.at[1])

    shape = (flat, 192)
    spot = 24 * lax.rem(iota(shape, 0), 4) + iota(shape, 0) // 4
    high, low = split(tall[1])
    table = nn(nt(eye_b, high).astype(BF), ones_at(iota(shape, 1) == spot))
    table = table + nn(nt(eye_b, low).astype(BF), ones_at(iota(shape, 1) == spot + 96))
    wl[...] = table.astype(BF)

    for group in GROUPS:
        for p in group:
            turned[p] = nn(wv[...], stacked_of(p))
            if p not in GROUPS[0]:
                xs[p] = nn(wp[...], stacked_of(p))
    for group in GROUPS:
        for p, total in star_block(turned, group):
            integ[p] = dofs[p * BASIS:(p + 1) * BASIS, :] + 0.25 * total

    def flux_block(j, side, first, read):
        totals = [None] * 3
        for q in range(QUANT):
            value = read(q)
            for i in range(3):
                r = ((j * 2 + side) * QUANT + first + i) * QUANT + q
                term = flux[r:r + 1, :] * value
                totals[i] = term if totals[i] is None else totals[i] + term
        return totals

    loads[2].wait()
    for j in range(4):
        for first in range(0, QUANT, 3):
            for i, total in enumerate(flux_block(j, 0, first, lambda q: xs[q, 32 * j:32 * j + 24, :])):
                comb[first + i, 24 * j:24 * j + 24, :] = total

    unpack(rest_copies, grecv, REST_PAIRS)
    for j in range(4):
        neighbours(j, HEAD, ALL)
        nvals[j, 6] = nvals[j, 3] - nvals[j, DIFF]
    for j in range(4):
        for first in range(0, QUANT, 3):
            for i, total in enumerate(flux_block(j, 1, first, lambda q: nvals[j, q])):
                spot = (first + i, slice(24 * j, 24 * j + 24))
                comb[spot[0], spot[1], :] = comb[spot[0], spot[1], :] + total

    pushed = nt(jnp.concatenate([slip_high[0:32], slip_low[0:32]], axis=0), oht[...])
    pushed = 2.0 * (pushed[0:24] + pushed[32:56])
    for j in range(4):
        spot = slice(24 * j, 24 * j + 24)
        part = pushed[:, j * elems:(j + 1) * elems]
        comb[3, spot, :] = comb[3, spot, :] - part
        comb[6, spot, :] = comb[6, spot, :] + part

    def lifted(value):
        high, low = split(value)
        return nn(wl[...], jnp.concatenate([high, high], axis=0)) + nn(wl[:, 0:96], low)

    for p in range(QUANT):
        out[p * BASIS:(p + 1) * BASIS, :] = integ[p] + 0.25 * lifted(comb[p])

    exchange_wait(1, vsend, vrecv, v_sem, loc_sem.at[1])
    high, low = split(vrecv[...])
    both = ones_at(iota(square, 0) == part_row)
    own = nn(nt(eye_p, high).astype(BF), both) + nn(nt(eye_p, low).astype(BF), both)
    slip_out[...] = jnp.where(rank_row == 0, own[0:FACE], own[64:64 + FACE])

    for copy in head_copies + rest_copies:
        copy.wait_send()
    exchange_end(2, qsend, q_sem)
    exchange_end(1, vsend, v_sem)


def store_results(dofs_ref, slip_ref, dofs_out, slip_out, sem):
    copies = [
        pltpu.make_async_copy(source, target, sem.at[n])
        for n, (source, target) in enumerate(((dofs_ref, dofs_out), (slip_ref, slip_out)))
    ]
    for copy in copies:
        copy.start()
    for copy in copies:
        copy.wait()


def solution(mesh):
    n_row, n_col = mesh.shape["row"], mesh.shape["col"]
    devices = n_row * n_col

    def per_device(dofs, star, flux, kxi, proj, lift, orient, nbr, ocode, slist, fpart, fitem, sh0, nm0, stv, slp):
        elems = dofs.shape[1]
        vmem, anywhere = pl.BlockSpec(memory_space=pltpu.VMEM), pl.BlockSpec(memory_space=pl.ANY)
        table = pltpu.VMEM((devices, 128), F32)
        pair = pltpu.SemaphoreType.DMA((2,))
        four = pltpu.SemaphoreType.DMA((4,))
        inside = pl.pallas_call(
            lambda *refs: kernel(n_row, n_col, *refs),
            out_shape=(pltpu.VMEM(dofs.shape, F32), pltpu.VMEM(slp.shape, F32)),
            in_specs=[anywhere] * 3 + [vmem] * 13,
            out_specs=(vmem, vmem),
            scratch_shapes=[
                pltpu.VMEM(dofs.shape, F32),
                pltpu.VMEM(star.shape, F32),
                pltpu.VMEM(flux.shape, F32),
                pltpu.VMEM((3 * BASIS, 192), BF),
                pltpu.VMEM((3 * BASIS, 192), BF),
                pltpu.VMEM((128, 192), BF),
                pltpu.VMEM((288, 192), F32),
                pltpu.VMEM((288, 192), BF),
                pltpu.VMEM((2, 4 * FACE, BASIS), F32),
                pltpu.VMEM((BASIS, 192), BF),
                pltpu.VMEM((2, QUANT, 3 * BASIS, elems), F32),
                pltpu.VMEM((QUANT, BASIS, elems), F32),
                pltpu.VMEM((len(BLOCKS) * 128, elems), BF),
                pltpu.VMEM((QUANT, 128, elems), F32),
                pltpu.VMEM((4, QUANT * 128, elems), BF),
                pltpu.VMEM((QUANT * 128, elems), BF),
                pltpu.VMEM((4, len(BLOCKS), 24, elems), F32),
                pltpu.VMEM((QUANT, 96, elems), F32),
                pltpu.VMEM((64, 4 * elems), F32),
                pltpu.VMEM((4 * elems, 2 * devices), BF),
                pltpu.VMEM((128, 128), F32),
                pltpu.VMEM((4, len(REST_PAIRS), BASIS, 128), F32),
                pltpu.VMEM((4, len(REST_PAIRS), BASIS, 128), F32),
                pltpu.VMEM((4, len(HEAD_PAIRS), BASIS, 128), F32),
                pltpu.VMEM((4, len(HEAD_PAIRS), BASIS, 128), F32),
                pltpu.VMEM((2 * devices, 128), F32),
                pltpu.VMEM((2 * devices, 128), F32),
                table, table,
                four, four, four, four, pair, pair, pair,
                pltpu.SemaphoreType.DMA((3,)),
            ],
            compiler_params=pltpu.CompilerParams(collective_id=0, has_side_effects=True),
        )(
            dofs, star, flux, kxi, jnp.transpose(proj, (2, 0, 1)), jnp.transpose(lift, (1, 0, 2)), orient,
            nbr, ocode, slist, fpart.reshape(1, -1), fitem.reshape(1, -1), sh0, nm0, stv, slp,
        )
        return pl.pallas_call(
            store_results,
            out_shape=(jax.ShapeDtypeStruct(dofs.shape, F32), jax.ShapeDtypeStruct(slp.shape, F32)),
            in_specs=[vmem] * 2,
            out_specs=(anywhere, anywhere),
            scratch_shapes=[pair],
            compiler_params=pltpu.CompilerParams(vmem_limit_bytes=1024 * 1024),
        )(*inside)

    split_cols = P(None, ("row", "col"))
    placed = (
        (split_cols,) * 3
        + (P(),) * 4
        + (split_cols,) * 3
        + (P(("row", "col"), None), P(("row", "col")))
        + (split_cols,) * 4
    )
    return jax.shard_map(
        per_device, mesh=mesh, in_specs=placed, out_specs=(split_cols, split_cols), check_vma=False
    )
```

```python
import jax
import jax.numpy as jnp
from jax import lax
from jax.experimental import pallas as pl
from jax.experimental.pallas import tpu as pltpu
from jax.sharding import PartitionSpec as P

QUANT = 9
BASIS = 56
FACE = 21
ORDER = 6
NEWTON_ITERS = 3
TIME_STEP = 2.0
FRIC_A = 0.5
MESH = pl.DeviceIdType.MESH
LOGICAL = pl.DeviceIdType.LOGICAL
BF = jnp.bfloat16
F32 = jnp.float32

DIFF = 9
BLOCKS = (0, DIFF, 3, 1, 2, 4, 5, 7, 8, 6)
GROUPS = ((0, 3, 6), (1, 2, 4), (5, 7, 8))
HEAD, ALL = 2 * 128, 9 * 128
HEAD_PAIRS = ((0, DIFF),)
REST_PAIRS = ((3, 1), (2, 4), (5, 7), (8, 8))
AT_SHEAR, AT_NORMAL, AT_STATE, AT_SLIP, AT_ITEM = 0, 24, 48, 72, 96


def iota(shape, dim):
    return lax.broadcasted_iota(jnp.int32, shape, dim)


def ones_at(mask):
    return jnp.where(mask, 1.0, 0.0).astype(BF)


def nn(a, b):
    return jnp.dot(a, b, preferred_element_type=F32)


def nt(a, b):
    return lax.dot_general(a, b, (((1,), (1,)), ((), ())), preferred_element_type=F32)


def split(x):
    high = x.astype(BF)
    return high, (x - high.astype(F32)).astype(BF)


def eye(rows, cols):
    return ones_at(iota((rows, cols), 0) == iota((rows, cols), 1))


def place(rows, cols, offsets):
    delta = iota((rows, cols), 1) - iota((rows, cols), 0)
    mask = delta == offsets[0]
    for offset in offsets[1:]:
        mask = mask | (delta == offset)
    return ones_at(mask)


def padded(x):
    return jnp.concatenate([x, jnp.zeros((8, x.shape[1]), F32)], axis=0)


def stacked(x):
    high, low = split(x)
    return jnp.concatenate([high, high, low], axis=0)


def inverse_sinh(value):
    magnitude = jnp.abs(value)
    squared = magnitude * magnitude
    positive = jnp.log1p(magnitude + squared / (1.0 + jnp.sqrt(1.0 + squared)))
    return jnp.where(value < 0.0, -positive, positive)


def friction_solve(shear, normal, shear_init, normal_init, state_var, slip_prev):
    shear_total = shear_init + shear
    normal_eff = normal_init * (1.0 + 0.5 * jnp.tanh(normal))
    growth = jnp.exp(state_var / FRIC_A) * 0.5
    slip_now = slip_prev
    for _ in range(NEWTON_ITERS):
        scaled = growth * slip_now
        misfit = shear_total - slip_now - FRIC_A * normal_eff * inverse_sinh(scaled)
        slope_val = -1.0 - FRIC_A * normal_eff * growth / jnp.sqrt(1.0 + scaled * scaled)
        slip_now = slip_now - misfit / slope_val
    return slip_now


def kernel(
    n_row, n_col,
    dofs_in, star_in, flux_in, kxi_in, proj_in, lift_in, orient_in, nbr_in, ocode_in, slist_in, fpart_in, fitem_in,
    sh0_in, nm0_in, stv_in, slp_in,
    out, slip_out,
    dofs, star, flux, kxi, proj, lift, orient, nbr, ocode, slist, fpart, fitem, sh0, nm0, stv, slp,
    wk, wv, wp, wo, w12, tall, wl, adv, integ, ihl, xs, glb, gtab, nvals, comb, fvals, oht, params,
    gsend, grecv, hsend, hrecv, qsend, qrecv, vsend, vrecv,
    gs_sem, gr_sem, hs_sem, hr_sem, q_sem, v_sem, loc_sem, in_sem,
):
    devices = n_row * n_col
    loads = [
        pltpu.make_async_copy(source, target, in_sem.at[n])
        for n, (source, target) in enumerate(
            (
                (dofs_in, dofs), (star_in, star), (flux_in, flux), (kxi_in, kxi), (proj_in, proj), (lift_in, lift),
                (orient_in, orient), (nbr_in, nbr), (ocode_in, ocode), (slist_in, slist), (fpart_in, fpart),
                (fitem_in, fitem), (sh0_in, sh0), (nm0_in, nm0), (stv_in, stv), (slp_in, slp),
            )
        )
    ]
    for load in loads[3:] + loads[0:3]:
        load.start()
    row, col = lax.axis_index("row"), lax.axis_index("col")
    me = row * n_col + col

    barrier = pltpu.get_barrier_semaphore()

    def ring(at, size, scale):
        return [lax.rem(at + step, size) * scale for step in range(size)]

    across = ring(row, n_row, n_col)
    deep = ring(col // 8, 4, 8)
    wide = ring(lax.rem(col, 8) // 2, 4, 2)
    core = ring(lax.rem(col, 2), 2, 1)
    hops = (0, 1, 2, 1)
    steps = [(y, z, x, c) for y in range(4) for z in range(4) for x in range(4) for c in range(2)][1:]
    steps.sort(key=lambda at: -(hops[at[0]] + hops[at[1]] + hops[at[2]]))

    def partner(at):
        return (across[at[0]] + deep[at[1]]) + (wide[at[2]] + core[at[3]])

    for at in steps:
        pl.semaphore_signal(barrier, inc=1, device_id=partner(at), device_id_type=LOGICAL)

    def own_copy(n, send, recv, local_sem):
        mine = pl.ds(n * me, n)
        return pltpu.make_async_copy(send.at[mine], recv.at[mine], local_sem)

    def exchange_start(n, send, recv, sem, local_sem):
        for at in steps:
            p = partner(at)
            pltpu.make_async_remote_copy(
                src_ref=send.at[pl.ds(n * p, n)],
                dst_ref=recv.at[pl.ds(n * me, n)],
                send_sem=sem.at[0],
                recv_sem=sem.at[1],
                device_id=p,
                device_id_type=LOGICAL,
            ).start()
        own_copy(n, send, recv, local_sem).start()

    def exchange_wait(n, send, recv, sem, local_sem):
        part = pl.ds(0, n * (devices - 1))
        pltpu.make_async_copy(recv.at[part], recv.at[part], sem.at[1]).wait()
        own_copy(n, send, recv, local_sem).wait()

    def exchange_end(n, send, sem):
        part = pl.ds(0, n * (devices - 1))
        pltpu.make_async_copy(send.at[part], send.at[part], sem.at[0]).wait()

    for load in loads[3:]:
        load.wait()

    at_high, at_low = place(BASIS, 192, (0, 128)), place(BASIS, 192, (64,))
    eye_b = eye(BASIS, BASIS)
    back, forth = [], []
    for d in range(3):
        high, low = split(kxi[d])
        forth.append(nn(high, at_high) + nn(low, at_low))
        back.append(nn(nt(eye_b, high).astype(BF), at_high) + nn(nt(eye_b, low).astype(BF), at_low))
    wk[...] = jnp.concatenate(back, axis=0).astype(BF)
    wv[...] = jnp.concatenate(forth, axis=0).astype(BF)
    square = (devices, fitem.shape[1])
    part_row = fpart[...]
    wide_part = jnp.sum(jnp.where(iota(square, 0) == iota(square, 1), part_row, 0), axis=1, keepdims=True)
    earlier = (wide_part == part_row) & (iota(square, 0) < iota(square, 1))
    rank_row = jnp.sum(jnp.where(earlier, 1, 0), axis=0, keepdims=True)
    tall_square = (2 * devices, fitem.shape[1])
    slot_of = ones_at(iota(tall_square, 0) == 2 * part_row + rank_row)
    params[...] = jnp.zeros_like(params)
    for at, table in ((AT_SHEAR, sh0), (AT_NORMAL, nm0), (AT_STATE, stv), (AT_SLIP, slp)):
        params[at:at + FACE, :] = table[...]
    params[AT_ITEM:AT_ITEM + 1, :] = (fitem[...] + 1).astype(F32)
    high, low = split(params[...])
    qsend[...] = nt(slot_of, high) + nt(slot_of, low)

    def put(weights, value, target, q):
        target[q] = nn(weights[...], stacked(padded(value)))

    loads[0].wait()
    loads[1].wait()
    for q in (0, 3, 6, 1, 2, 4, 5, 7, 8):
        start = dofs[q * BASIS:(q + 1) * BASIS, :]
        integ[q] = TIME_STEP * start
        put(wk, start, adv.at[0], q)

    def star_block(source, group):
        sides = []
        for lanes in (slice(0, 128), slice(128, 256)):
            totals = [None] * 3
            for q in (0, 3, 6, 1, 2, 4, 5, 7, 8):
                for d in range(3):
                    value = source[q, d * BASIS:(d + 1) * BASIS, lanes]
                    for i, p in enumerate(group):
                        r = (d * QUANT + p) * QUANT + q
                        term = star[r:r + 1, lanes] * value
                        totals[i] = term if totals[i] is None else totals[i] + term
            sides.append(totals)
        return [(p, jnp.concatenate([left, right], axis=1)) for p, left, right in zip(group, *sides)]

    factor = TIME_STEP
    for k in range(1, ORDER - 1):
        if k == 3:
            pl.semaphore_wait(barrier, devices - 1)
            exchange_start(2, qsend, qrecv, q_sem, loc_sem.at[0])
        factor = factor * TIME_STEP / (k + 1)
        source, target = adv.at[(k - 1) % 2], adv.at[k % 2]
        for group in GROUPS:
            for p, total in star_block(source, group):
                integ[p] = integ[p] + factor * total
                put(wk, total, target, p)
    factor = factor * TIME_STEP / ORDER
    source, turned = adv.at[(ORDER - 2) % 2], adv.at[(ORDER - 1) % 2]

    small = slist.shape[1]
    elems = dofs.shape[1]
    spread = ones_at(lax.rem(iota((small, 4 * small), 1), small) == iota((small, 4 * small), 0))
    listed = nn(slist[...].astype(F32).astype(BF), spread)
    listed = jnp.sum(
        jnp.where(iota((4, 4 * small), 1) // small == iota((4, 4 * small), 0), listed, 0.0), axis=0, keepdims=True
    ).astype(jnp.int32)
    half = iota((BASIS, 128), 1) < 64
    targets = (
        lax.rem(row + 1, n_row) * n_col + col,
        lax.rem(row + n_row - 1, n_row) * n_col + col,
        row * n_col + lax.rem(col + 1, n_col),
        row * n_col + lax.rem(col + n_col - 1, n_col),
    )

    def ghost_copies(send, recv, send_sem, recv_sem):
        return [
            pltpu.make_async_remote_copy(
                src_ref=send.at[d],
                dst_ref=recv.at[d],
                send_sem=send_sem.at[d],
                recv_sem=recv_sem.at[d],
                device_id=targets[d],
                device_id_type=LOGICAL,
            )
            for d in range(4)
        ]

    head_copies = ghost_copies(hsend, hrecv, hs_sem, hr_sem)
    rest_copies = ghost_copies(gsend, grecv, gs_sem, gr_sem)

    def pack(send, pairs, start, stop):
        picked = nn(ihl[start:stop, :], ones_at(iota((elems, 4 * small), 0) == listed))
        for side in range(2):
            lanes = slice(side * 128, side * 128 + 128)
            for n, pair in enumerate(pairs):
                ends = []
                for q in pair:
                    at = BLOCKS.index(q) * 128 - start
                    ends.append(picked[at:at + BASIS, lanes] + picked[at + 64:at + 64 + BASIS, lanes])
                first, second = ends
                send[2 * side, n] = jnp.where(half, first, pltpu.roll(second, 64, 1))
                send[2 * side + 1, n] = jnp.where(half, pltpu.roll(first, 64, 1), second)

    def finish(group):
        values = {p: integ[p] + factor * total for p, total in star_block(source, group)}
        if group == GROUPS[0]:
            values[DIFF] = values[3] - values[6]
        for p, value in values.items():
            high, low = split(padded(value))
            block = BLOCKS.index(p) * 128
            ihl[block:block + 64, :] = high
            ihl[block + 64:block + 128, :] = low

    def stacked_of(p):
        block = BLOCKS.index(p) * 128
        high = ihl[block:block + 64, :]
        return jnp.concatenate([high, high, ihl[block + 64:block + 128, :]], axis=0)

    finish(GROUPS[0])
    pack(hsend, HEAD_PAIRS, 0, HEAD)
    for copy in head_copies:
        copy.start()

    flat = 4 * FACE
    for g in range(FACE):
        tall[0, 4 * g:4 * g + 4, :] = proj[g]
        tall[1, 4 * g:4 * g + 4, :] = lift[g]
    shape = (128, flat)
    order = ones_at((iota(shape, 0) // 32 + 4 * lax.rem(iota(shape, 0), 32)) == iota(shape, 1))
    high, low = split(tall[0])
    proj_high, proj_low = nn(order, high).astype(BF), nn(order, low).astype(BF)
    wp[...] = (nn(proj_high, at_high) + nn(proj_low, at_low)).astype(BF)
    rows = []
    pick_g = eye(24, FACE)
    turn_high, turn_low = place(FACE, 96, (0, 64)), place(FACE, 96, (32,))
    for o in range(3):
        high, low = split(orient[o])
        rows.append(nn(nt(pick_g, high).astype(BF), turn_high) + nn(nt(pick_g, low).astype(BF), turn_low))
    turn = jnp.concatenate(rows, axis=0).astype(BF)
    for j in range(4):
        own_rows = slice(32 * j, 32 * j + 32)
        both = jnp.concatenate([proj_high[own_rows], proj_high[own_rows], proj_low[own_rows]], axis=0)
        high, low = split(nn(turn, both))
        wo[72 * j:72 * j + 72, :] = nn(high, at_high) + nn(low, at_low)
    w12[...] = wo[...].astype(BF)
    for p in GROUPS[0]:
        xs[p] = nn(wp[...], stacked_of(p))
    finish(GROUPS[1])
    finish(GROUPS[2])
    pack(gsend, REST_PAIRS, HEAD, ALL)
    for copy in rest_copies:
        copy.start()

    square_e = (elems, elems)
    for j in range(4):
        seen = nbr[j:j + 1, :]
        key = jnp.where(seen < 4 * elems, seen & (elems - 1), -1)
        glb[j] = nn(ihl[0:ALL, :], ones_at(iota(square_e, 0) == key)).astype(BF)

    exchange_wait(2, qsend, qrecv, q_sem, loc_sem.at[0])
    eye_p = eye(128, 128)
    high, low = split(qrecv[...])
    asked = nt(eye_p, high) + nt(eye_p, low)
    slots = 2 * devices
    item = asked[AT_ITEM:AT_ITEM + 1].astype(jnp.int32) - 1
    oht[...] = ones_at(iota((4 * elems, slots), 0) == item)

    inside = (row > 0, row < n_row - 1, col > 0, col < n_col - 1)

    def unpack(copies, recv, pairs):
        for copy in copies:
            copy.wait_recv()
        for side in range(2):
            lanes = slice(side * 128, side * 128 + 128)
            for n, pair in enumerate(pairs):
                first = jnp.where(inside[2 * side], recv[2 * side, n], 0.0)
                second = jnp.where(inside[2 * side + 1], recv[2 * side + 1, n], 0.0)
                halves = [(pair[0], jnp.where(half, first, pltpu.roll(second, 64, 1)))]
                if pair[1] != pair[0]:
                    halves.append((pair[1], jnp.where(half, pltpu.roll(first, 64, 1), second)))
                for quant, value in halves:
                    high, low = split(padded(value))
                    block = BLOCKS.index(quant) * 128
                    gtab[block:block + 64, lanes] = high
                    gtab[block + 64:block + 128, lanes] = low

    unpack(head_copies, hrecv, HEAD_PAIRS)

    def neighbours(j, start, stop):
        seen = nbr[j:j + 1, :]
        key = jnp.where(seen < 4 * elems, -1, seen & (elems - 1))
        code = 3 * (lax.shift_right_logical(seen, 8) & 3) + ocode[j:j + 1, :]
        got = nn(gtab[start:stop, :], ones_at(iota(square_e, 0) == key)).astype(BF) + glb[j, start:stop, :]
        for block in range(start // 128, stop // 128):
            at = block * 128 - start
            high, low = got[at:at + 64], got[at + 64:at + 128]
            turns = nn(w12[...], jnp.concatenate([high, high, low], axis=0))
            value = turns[0:24]
            for c in range(1, 12):
                value = jnp.where(code == c, turns[24 * c:24 * c + 24], value)
            nvals[j, BLOCKS[block]] = value

    fvals[...] = jnp.zeros_like(fvals)
    for j in range(4):
        neighbours(j, 0, HEAD)
        lanes = slice(j * elems, (j + 1) * elems)
        x0, x3, x6 = (xs[q, 32 * j:32 * j + 24, :] for q in (0, 3, 6))
        fvals[0:24, lanes] = 0.5 * (x3 + x6) + 0.5 * nvals[j, DIFF]
        fvals[24:48, lanes] = 0.5 * (x0 + nvals[j, 0])

    high, low = split(fvals[...])
    held = nn(high, oht[...]) + nn(low, oht[...])
    slip = friction_solve(
        held[0:FACE],
        held[24:24 + FACE],
        asked[AT_SHEAR:AT_SHEAR + FACE],
        asked[AT_NORMAL:AT_NORMAL + FACE],
        asked[AT_STATE:AT_STATE + FACE],
        asked[AT_SLIP:AT_SLIP + FACE],
    )
    slip = jnp.concatenate([slip, jnp.zeros((64 - FACE, slots), F32)], axis=0)
    slip_high, slip_low = split(slip)
    going = jnp.zeros((devices, 128), F32)
    blank = jnp.zeros((64, slots), BF)
    for k in range(2):
        owner = ones_at(iota((devices, slots), 1) == 2 * iota((devices, slots), 0) + k)
        for part in (slip_high, slip_low):
            going = going + nt(owner, jnp.concatenate([part, blank] if k == 0 else [blank, part], axis=0))
    vsend[...] = going
    exchange_start(1, vsend, vrecv, v_sem, loc_sem.at[1])

    shape = (flat, 192)
    spot = 24 * lax.rem(iota(shape, 0), 4) + iota(shape, 0) // 4
    high, low = split(tall[1])
    table = nn(nt(eye_b, high).astype(BF), ones_at(iota(shape, 1) == spot))
    table = table + nn(nt(eye_b, low).astype(BF), ones_at(iota(shape, 1) == spot + 96))
    wl[...] = table.astype(BF)

    for group in GROUPS:
        for p in group:
            turned[p] = nn(wv[...], stacked_of(p))
            if p not in GROUPS[0]:
                xs[p] = nn(wp[...], stacked_of(p))
    for group in GROUPS:
        for p, total in star_block(turned, group):
            integ[p] = dofs[p * BASIS:(p + 1) * BASIS, :] + 0.25 * total

    def flux_block(j, side, first, read):
        totals = [None] * 3
        for q in range(QUANT):
            value = read(q)
            for i in range(3):
                r = ((j * 2 + side) * QUANT + first + i) * QUANT + q
                term = flux[r:r + 1, :] * value
                totals[i] = term if totals[i] is None else totals[i] + term
        return totals

    loads[2].wait()
    for j in range(4):
        for first in range(0, QUANT, 3):
            for i, total in enumerate(flux_block(j, 0, first, lambda q: xs[q, 32 * j:32 * j + 24, :])):
                comb[first + i, 24 * j:24 * j + 24, :] = total

    unpack(rest_copies, grecv, REST_PAIRS)
    for j in range(4):
        neighbours(j, HEAD, ALL)
        nvals[j, 6] = nvals[j, 3] - nvals[j, DIFF]
    for j in range(4):
        for first in range(0, QUANT, 3):
            for i, total in enumerate(flux_block(j, 1, first, lambda q: nvals[j, q])):
                spot = (first + i, slice(24 * j, 24 * j + 24))
                comb[spot[0], spot[1], :] = comb[spot[0], spot[1], :] + total

    pushed = nt(jnp.concatenate([slip_high[0:32], slip_low[0:32]], axis=0), oht[...])
    pushed = 2.0 * (pushed[0:24] + pushed[32:56])
    for j in range(4):
        spot = slice(24 * j, 24 * j + 24)
        part = pushed[:, j * elems:(j + 1) * elems]
        comb[3, spot, :] = comb[3, spot, :] - part
        comb[6, spot, :] = comb[6, spot, :] + part

    def lifted(value):
        high, low = split(value)
        return nn(wl[...], jnp.concatenate([high, high], axis=0)) + nn(wl[:, 0:96], low)

    for p in range(QUANT):
        out[p * BASIS:(p + 1) * BASIS, :] = integ[p] + 0.25 * lifted(comb[p])

    exchange_wait(1, vsend, vrecv, v_sem, loc_sem.at[1])
    high, low = split(vrecv[...])
    both = ones_at(iota(square, 0) == part_row)
    own = nn(nt(eye_p, high).astype(BF), both) + nn(nt(eye_p, low).astype(BF), both)
    slip_out[...] = jnp.where(rank_row == 0, own[0:FACE], own[64:64 + FACE])

    for copy in head_copies + rest_copies:
        copy.wait_send()
    exchange_end(2, qsend, q_sem)
    exchange_end(1, vsend, v_sem)


def store_results(dofs_ref, slip_ref, dofs_out, slip_out, sem):
    copies = [
        pltpu.make_async_copy(source, target, sem.at[n])
        for n, (source, target) in enumerate(((dofs_ref, dofs_out), (slip_ref, slip_out)))
    ]
    for copy in copies:
        copy.start()
    for copy in copies:
        copy.wait()


def solution(mesh):
    n_row, n_col = mesh.shape["row"], mesh.shape["col"]
    devices = n_row * n_col

    def per_device(dofs, star, flux, kxi, proj, lift, orient, nbr, ocode, slist, fpart, fitem, sh0, nm0, stv, slp):
        elems = dofs.shape[1]
        vmem, anywhere = pl.BlockSpec(memory_space=pltpu.VMEM), pl.BlockSpec(memory_space=pl.ANY)
        table = pltpu.VMEM((devices, 128), F32)
        pair = pltpu.SemaphoreType.DMA((2,))
        four = pltpu.SemaphoreType.DMA((4,))
        operands = (
            dofs, star, flux, kxi, jnp.transpose(proj, (2, 0, 1)), jnp.transpose(lift, (1, 0, 2)), orient,
            nbr, ocode, slist, fpart.reshape(1, -1), fitem.reshape(1, -1), sh0, nm0, stv, slp,
        )
        inside = pl.pallas_call(
            lambda *refs: kernel(n_row, n_col, *refs),
            out_shape=(pltpu.VMEM(dofs.shape, F32), pltpu.VMEM(slp.shape, F32)),
            in_specs=[anywhere] * 16,
            out_specs=(vmem, vmem),
            scratch_shapes=[
                *(pltpu.VMEM(operand.shape, operand.dtype) for operand in operands),
                pltpu.VMEM((3 * BASIS, 192), BF),
                pltpu.VMEM((3 * BASIS, 192), BF),
                pltpu.VMEM((128, 192), BF),
                pltpu.VMEM((288, 192), F32),
                pltpu.VMEM((288, 192), BF),
                pltpu.VMEM((2, 4 * FACE, BASIS), F32),
                pltpu.VMEM((BASIS, 192), BF),
                pltpu.VMEM((2, QUANT, 3 * BASIS, elems), F32),
                pltpu.VMEM((QUANT, BASIS, elems), F32),
                pltpu.VMEM((len(BLOCKS) * 128, elems), BF),
                pltpu.VMEM((QUANT, 128, elems), F32),
                pltpu.VMEM((4, QUANT * 128, elems), BF),
                pltpu.VMEM((QUANT * 128, elems), BF),
                pltpu.VMEM((4, len(BLOCKS), 24, elems), F32),
                pltpu.VMEM((QUANT, 96, elems), F32),
                pltpu.VMEM((64, 4 * elems), F32),
                pltpu.VMEM((4 * elems, 2 * devices), BF),
                pltpu.VMEM((128, 128), F32),
                pltpu.VMEM((4, len(REST_PAIRS), BASIS, 128), F32),
                pltpu.VMEM((4, len(REST_PAIRS), BASIS, 128), F32),
                pltpu.VMEM((4, len(HEAD_PAIRS), BASIS, 128), F32),
                pltpu.VMEM((4, len(HEAD_PAIRS), BASIS, 128), F32),
                pltpu.VMEM((2 * devices, 128), F32),
                pltpu.VMEM((2 * devices, 128), F32),
                table, table,
                four, four, four, four, pair, pair, pair,
                pltpu.SemaphoreType.DMA((16,)),
            ],
            compiler_params=pltpu.CompilerParams(collective_id=0, has_side_effects=True),
        )(*operands)
        return pl.pallas_call(
            store_results,
            out_shape=(jax.ShapeDtypeStruct(dofs.shape, F32), jax.ShapeDtypeStruct(slp.shape, F32)),
            in_specs=[vmem] * 2,
            out_specs=(anywhere, anywhere),
            scratch_shapes=[pair],
            compiler_params=pltpu.CompilerParams(vmem_limit_bytes=1024 * 1024),
        )(*inside)

    split_cols = P(None, ("row", "col"))
    placed = (
        (split_cols,) * 3
        + (P(),) * 4
        + (split_cols,) * 3
        + (P(("row", "col"), None), P(("row", "col")))
        + (split_cols,) * 4
    )
    return jax.shard_map(
        per_device, mesh=mesh, in_specs=placed, out_specs=(split_cols, split_cols), check_vma=False
    )
```

```python
import jax
import jax.numpy as jnp
from jax import lax
from jax.experimental import pallas as pl
from jax.experimental.pallas import tpu as pltpu
from jax.sharding import PartitionSpec as P

QUANT = 9
BASIS = 56
FACE = 21
ORDER = 6
NEWTON_ITERS = 3
TIME_STEP = 2.0
FRIC_A = 0.5
MESH = pl.DeviceIdType.MESH
LOGICAL = pl.DeviceIdType.LOGICAL
BF = jnp.bfloat16
F32 = jnp.float32

DIFF = 9
BLOCKS = (0, DIFF, 3, 1, 2, 4, 5, 7, 8, 6)
GROUPS = ((0, 3, 6), (1, 2, 4), (5, 7, 8))
HEAD, ALL = 2 * 128, 9 * 128
HEAD_PAIRS = ((0, DIFF),)
REST_PAIRS = ((3, 1), (2, 4), (5, 7), (8, 8))
AT_SHEAR, AT_NORMAL, AT_STATE, AT_SLIP, AT_ITEM = 0, 24, 48, 72, 96


def iota(shape, dim):
    return lax.broadcasted_iota(jnp.int32, shape, dim)


def ones_at(mask):
    return jnp.where(mask, 1.0, 0.0).astype(BF)


def nn(a, b):
    return jnp.dot(a, b, preferred_element_type=F32)


def nt(a, b):
    return lax.dot_general(a, b, (((1,), (1,)), ((), ())), preferred_element_type=F32)


def split(x):
    high = x.astype(BF)
    return high, (x - high.astype(F32)).astype(BF)


def eye(rows, cols):
    return ones_at(iota((rows, cols), 0) == iota((rows, cols), 1))


def place(rows, cols, offsets):
    delta = iota((rows, cols), 1) - iota((rows, cols), 0)
    mask = delta == offsets[0]
    for offset in offsets[1:]:
        mask = mask | (delta == offset)
    return ones_at(mask)


def padded(x):
    return jnp.concatenate([x, jnp.zeros((8, x.shape[1]), F32)], axis=0)


def stacked(x):
    high, low = split(x)
    return jnp.concatenate([high, high, low], axis=0)


def inverse_sinh(value):
    magnitude = jnp.abs(value)
    squared = magnitude * magnitude
    positive = jnp.log1p(magnitude + squared / (1.0 + jnp.sqrt(1.0 + squared)))
    return jnp.where(value < 0.0, -positive, positive)


def friction_solve(shear, normal, shear_init, normal_init, state_var, slip_prev):
    shear_total = shear_init + shear
    normal_eff = normal_init * (1.0 + 0.5 * jnp.tanh(normal))
    growth = jnp.exp(state_var / FRIC_A) * 0.5
    slip_now = slip_prev
    for _ in range(NEWTON_ITERS):
        scaled = growth * slip_now
        misfit = shear_total - slip_now - FRIC_A * normal_eff * inverse_sinh(scaled)
        slope_val = -1.0 - FRIC_A * normal_eff * growth / jnp.sqrt(1.0 + scaled * scaled)
        slip_now = slip_now - misfit / slope_val
    return slip_now


def kernel(
    n_row, n_col,
    dofs_in, star_in, flux_in, kxi_in, proj_in, lift_in, orient_in, nbr_in, ocode_in, slist_in, fpart_in, fitem_in,
    sh0_in, nm0_in, stv_in, slp_in,
    out, slip_out,
    dofs, star, flux, kxi, proj, lift, orient, nbr, ocode, slist, fpart, fitem, sh0, nm0, stv, slp,
    wk, wv, wp, wo, w12, tall, wl, adv, integ, ihl, xs, glb, gtab, nvals, comb, fvals, oht, params,
    gsend, grecv, hsend, hrecv, qsend, qrecv, vsend, vrecv,
    gs_sem, gr_sem, hs_sem, hr_sem, q_sem, v_sem, loc_sem, in_sem,
):
    devices = n_row * n_col
    loads = [
        pltpu.make_async_copy(source, target, in_sem.at[n])
        for n, (source, target) in enumerate(
            (
                (dofs_in, dofs), (star_in, star), (flux_in, flux), (kxi_in, kxi), (proj_in, proj), (lift_in, lift),
                (orient_in, orient), (nbr_in, nbr), (ocode_in, ocode), (slist_in, slist), (fpart_in, fpart),
                (fitem_in, fitem), (sh0_in, sh0), (nm0_in, nm0), (stv_in, stv), (slp_in, slp),
            )
        )
    ]
    for load in loads[3:] + loads[0:3]:
        load.start()
    row, col = lax.axis_index("row"), lax.axis_index("col")
    me = row * n_col + col

    barrier = pltpu.get_barrier_semaphore()

    def ring(at, size, scale):
        return [lax.rem(at + step, size) * scale for step in range(size)]

    across = ring(row, n_row, n_col)
    deep = ring(col // 8, 4, 8)
    wide = ring(lax.rem(col, 8) // 2, 4, 2)
    core = ring(lax.rem(col, 2), 2, 1)
    hops = (0, 1, 2, 1)
    steps = [(y, z, x, c) for y in range(4) for z in range(4) for x in range(4) for c in range(2)][1:]
    steps.sort(key=lambda at: -(hops[at[0]] + hops[at[1]] + hops[at[2]]))

    def partner(at):
        return (across[at[0]] + deep[at[1]]) + (wide[at[2]] + core[at[3]])

    for at in steps:
        pl.semaphore_signal(barrier, inc=1, device_id=partner(at), device_id_type=LOGICAL)

    def own_copy(n, send, recv, local_sem):
        mine = pl.ds(n * me, n)
        return pltpu.make_async_copy(send.at[mine], recv.at[mine], local_sem)

    def exchange_start(n, send, recv, sem, local_sem):
        for at in steps:
            p = partner(at)
            pltpu.make_async_remote_copy(
                src_ref=send.at[pl.ds(n * p, n)],
                dst_ref=recv.at[pl.ds(n * me, n)],
                send_sem=sem.at[0],
                recv_sem=sem.at[1],
                device_id=p,
                device_id_type=LOGICAL,
            ).start()
        own_copy(n, send, recv, local_sem).start()

    def exchange_wait(n, send, recv, sem, local_sem):
        part = pl.ds(0, n * (devices - 1))
        pltpu.make_async_copy(recv.at[part], recv.at[part], sem.at[1]).wait()
        own_copy(n, send, recv, local_sem).wait()

    def exchange_end(n, send, sem):
        part = pl.ds(0, n * (devices - 1))
        pltpu.make_async_copy(send.at[part], send.at[part], sem.at[0]).wait()

    for load in loads[3:]:
        load.wait()

    at_high, at_low = place(BASIS, 192, (0, 128)), place(BASIS, 192, (64,))
    eye_b = eye(BASIS, BASIS)
    back = []
    for d in range(3):
        high, low = split(kxi[d])
        back.append(nn(nt(eye_b, high).astype(BF), at_high) + nn(nt(eye_b, low).astype(BF), at_low))
    wk[...] = jnp.concatenate(back, axis=0).astype(BF)
    def put(weights, value, target, q):
        target[q] = nn(weights[...], stacked(padded(value)))

    loads[0].wait()
    loads[1].wait()
    for q in (0, 3, 6, 1, 2, 4, 5, 7, 8):
        start = dofs[q * BASIS:(q + 1) * BASIS, :]
        integ[q] = TIME_STEP * start
        put(wk, start, adv.at[0], q)

    def star_block(source, group):
        sides = []
        for lanes in (slice(0, 128), slice(128, 256)):
            totals = [None] * 3
            for q in (0, 3, 6, 1, 2, 4, 5, 7, 8):
                for d in range(3):
                    value = source[q, d * BASIS:(d + 1) * BASIS, lanes]
                    for i, p in enumerate(group):
                        r = (d * QUANT + p) * QUANT + q
                        term = star[r:r + 1, lanes] * value
                        totals[i] = term if totals[i] is None else totals[i] + term
            sides.append(totals)
        return [(p, jnp.concatenate([left, right], axis=1)) for p, left, right in zip(group, *sides)]

    square = (devices, fitem.shape[1])
    part_row = fpart[...]
    wide_part = jnp.sum(jnp.where(iota(square, 0) == iota(square, 1), part_row, 0), axis=1, keepdims=True)
    earlier = (wide_part == part_row) & (iota(square, 0) < iota(square, 1))
    rank_row = jnp.sum(jnp.where(earlier, 1, 0), axis=0, keepdims=True)
    tall_square = (2 * devices, fitem.shape[1])
    slot_of = ones_at(iota(tall_square, 0) == 2 * part_row + rank_row)
    params[...] = jnp.zeros_like(params)
    for at, table in ((AT_SHEAR, sh0), (AT_NORMAL, nm0), (AT_STATE, stv), (AT_SLIP, slp)):
        params[at:at + FACE, :] = table[...]
    params[AT_ITEM:AT_ITEM + 1, :] = (fitem[...] + 1).astype(F32)
    high, low = split(params[...])
    qsend[...] = nt(slot_of, high) + nt(slot_of, low)

    factor = TIME_STEP
    for k in range(1, ORDER - 1):
        if k == 3:
            pl.semaphore_wait(barrier, devices - 1)
            exchange_start(2, qsend, qrecv, q_sem, loc_sem.at[0])
        factor = factor * TIME_STEP / (k + 1)
        source, target = adv.at[(k - 1) % 2], adv.at[k % 2]
        for group in GROUPS:
            for p, total in star_block(source, group):
                integ[p] = integ[p] + factor * total
                put(wk, total, target, p)
    factor = factor * TIME_STEP / ORDER
    source, turned = adv.at[(ORDER - 2) % 2], adv.at[(ORDER - 1) % 2]

    small = slist.shape[1]
    elems = dofs.shape[1]
    spread = ones_at(lax.rem(iota((small, 4 * small), 1), small) == iota((small, 4 * small), 0))
    listed = nn(slist[...].astype(F32).astype(BF), spread)
    listed = jnp.sum(
        jnp.where(iota((4, 4 * small), 1) // small == iota((4, 4 * small), 0), listed, 0.0), axis=0, keepdims=True
    ).astype(jnp.int32)
    half = iota((BASIS, 128), 1) < 64
    targets = (
        lax.rem(row + 1, n_row) * n_col + col,
        lax.rem(row + n_row - 1, n_row) * n_col + col,
        row * n_col + lax.rem(col + 1, n_col),
        row * n_col + lax.rem(col + n_col - 1, n_col),
    )

    def ghost_copies(send, recv, send_sem, recv_sem):
        return [
            pltpu.make_async_remote_copy(
                src_ref=send.at[d],
                dst_ref=recv.at[d],
                send_sem=send_sem.at[d],
                recv_sem=recv_sem.at[d],
                device_id=targets[d],
                device_id_type=LOGICAL,
            )
            for d in range(4)
        ]

    head_copies = ghost_copies(hsend, hrecv, hs_sem, hr_sem)
    rest_copies = ghost_copies(gsend, grecv, gs_sem, gr_sem)

    def pack(send, pairs, start, stop):
        picked = nn(ihl[start:stop, :], ones_at(iota((elems, 4 * small), 0) == listed))
        for side in range(2):
            lanes = slice(side * 128, side * 128 + 128)
            for n, pair in enumerate(pairs):
                ends = []
                for q in pair:
                    at = BLOCKS.index(q) * 128 - start
                    ends.append(picked[at:at + BASIS, lanes] + picked[at + 64:at + 64 + BASIS, lanes])
                first, second = ends
                send[2 * side, n] = jnp.where(half, first, pltpu.roll(second, 64, 1))
                send[2 * side + 1, n] = jnp.where(half, pltpu.roll(first, 64, 1), second)

    def finish(group):
        values = {p: integ[p] + factor * total for p, total in star_block(source, group)}
        if group == GROUPS[0]:
            values[DIFF] = values[3] - values[6]
        for p, value in values.items():
            high, low = split(padded(value))
            block = BLOCKS.index(p) * 128
            ihl[block:block + 64, :] = high
            ihl[block + 64:block + 128, :] = low

    def stacked_of(p):
        block = BLOCKS.index(p) * 128
        high = ihl[block:block + 64, :]
        return jnp.concatenate([high, high, ihl[block + 64:block + 128, :]], axis=0)

    finish(GROUPS[0])
    pack(hsend, HEAD_PAIRS, 0, HEAD)
    for copy in head_copies:
        copy.start()

    forth = []
    for d in range(3):
        high, low = split(kxi[d])
        forth.append(nn(high, at_high) + nn(low, at_low))
    wv[...] = jnp.concatenate(forth, axis=0).astype(BF)
    flat = 4 * FACE
    for g in range(FACE):
        tall[0, 4 * g:4 * g + 4, :] = proj[g]
        tall[1, 4 * g:4 * g + 4, :] = lift[g]
    shape = (128, flat)
    order = ones_at((iota(shape, 0) // 32 + 4 * lax.rem(iota(shape, 0), 32)) == iota(shape, 1))
    high, low = split(tall[0])
    proj_high, proj_low = nn(order, high).astype(BF), nn(order, low).astype(BF)
    wp[...] = (nn(proj_high, at_high) + nn(proj_low, at_low)).astype(BF)
    rows = []
    pick_g = eye(24, FACE)
    turn_high, turn_low = place(FACE, 96, (0, 64)), place(FACE, 96, (32,))
    for o in range(3):
        high, low = split(orient[o])
        rows.append(nn(nt(pick_g, high).astype(BF), turn_high) + nn(nt(pick_g, low).astype(BF), turn_low))
    turn = jnp.concatenate(rows, axis=0).astype(BF)
    for j in range(4):
        own_rows = slice(32 * j, 32 * j + 32)
        both = jnp.concatenate([proj_high[own_rows], proj_high[own_rows], proj_low[own_rows]], axis=0)
        high, low = split(nn(turn, both))
        wo[72 * j:72 * j + 72, :] = nn(high, at_high) + nn(low, at_low)
    w12[...] = wo[...].astype(BF)
    for p in GROUPS[0]:
        xs[p] = nn(wp[...], stacked_of(p))
    finish(GROUPS[1])
    finish(GROUPS[2])
    pack(gsend, REST_PAIRS, HEAD, ALL)
    for copy in rest_copies:
        copy.start()

    square_e = (elems, elems)
    for j in range(4):
        seen = nbr[j:j + 1, :]
        key = jnp.where(seen < 4 * elems, seen & (elems - 1), -1)
        glb[j] = nn(ihl[0:ALL, :], ones_at(iota(square_e, 0) == key)).astype(BF)

    exchange_wait(2, qsend, qrecv, q_sem, loc_sem.at[0])
    eye_p = eye(128, 128)
    high, low = split(qrecv[...])
    asked = nt(eye_p, high) + nt(eye_p, low)
    slots = 2 * devices
    item = asked[AT_ITEM:AT_ITEM + 1].astype(jnp.int32) - 1
    oht[...] = ones_at(iota((4 * elems, slots), 0) == item)

    inside = (row > 0, row < n_row - 1, col > 0, col < n_col - 1)

    def unpack(copies, recv, pairs):
        for copy in copies:
            copy.wait_recv()
        for side in range(2):
            lanes = slice(side * 128, side * 128 + 128)
            for n, pair in enumerate(pairs):
                first = jnp.where(inside[2 * side], recv[2 * side, n], 0.0)
                second = jnp.where(inside[2 * side + 1], recv[2 * side + 1, n], 0.0)
                halves = [(pair[0], jnp.where(half, first, pltpu.roll(second, 64, 1)))]
                if pair[1] != pair[0]:
                    halves.append((pair[1], jnp.where(half, pltpu.roll(first, 64, 1), second)))
                for quant, value in halves:
                    high, low = split(padded(value))
                    block = BLOCKS.index(quant) * 128
                    gtab[block:block + 64, lanes] = high
                    gtab[block + 64:block + 128, lanes] = low

    unpack(head_copies, hrecv, HEAD_PAIRS)

    def neighbours(j, start, stop):
        seen = nbr[j:j + 1, :]
        key = jnp.where(seen < 4 * elems, -1, seen & (elems - 1))
        code = 3 * (lax.shift_right_logical(seen, 8) & 3) + ocode[j:j + 1, :]
        got = nn(gtab[start:stop, :], ones_at(iota(square_e, 0) == key)).astype(BF) + glb[j, start:stop, :]
        for block in range(start // 128, stop // 128):
            at = block * 128 - start
            high, low = got[at:at + 64], got[at + 64:at + 128]
            turns = nn(w12[...], jnp.concatenate([high, high, low], axis=0))
            value = turns[0:24]
            for c in range(1, 12):
                value = jnp.where(code == c, turns[24 * c:24 * c + 24], value)
            nvals[j, BLOCKS[block]] = value

    fvals[...] = jnp.zeros_like(fvals)
    for j in range(4):
        neighbours(j, 0, HEAD)
        lanes = slice(j * elems, (j + 1) * elems)
        x0, x3, x6 = (xs[q, 32 * j:32 * j + 24, :] for q in (0, 3, 6))
        fvals[0:24, lanes] = 0.5 * (x3 + x6) + 0.5 * nvals[j, DIFF]
        fvals[24:48, lanes] = 0.5 * (x0 + nvals[j, 0])

    high, low = split(fvals[...])
    held = nn(high, oht[...]) + nn(low, oht[...])
    slip = friction_solve(
        held[0:FACE],
        held[24:24 + FACE],
        asked[AT_SHEAR:AT_SHEAR + FACE],
        asked[AT_NORMAL:AT_NORMAL + FACE],
        asked[AT_STATE:AT_STATE + FACE],
        asked[AT_SLIP:AT_SLIP + FACE],
    )
    slip = jnp.concatenate([slip, jnp.zeros((64 - FACE, slots), F32)], axis=0)
    slip_high, slip_low = split(slip)
    going = jnp.zeros((devices, 128), F32)
    blank = jnp.zeros((64, slots), BF)
    for k in range(2):
        owner = ones_at(iota((devices, slots), 1) == 2 * iota((devices, slots), 0) + k)
        for part in (slip_high, slip_low):
            going = going + nt(owner, jnp.concatenate([part, blank] if k == 0 else [blank, part], axis=0))
    vsend[...] = going
    exchange_start(1, vsend, vrecv, v_sem, loc_sem.at[1])

    shape = (flat, 192)
    spot = 24 * lax.rem(iota(shape, 0), 4) + iota(shape, 0) // 4
    high, low = split(tall[1])
    table = nn(nt(eye_b, high).astype(BF), ones_at(iota(shape, 1) == spot))
    table = table + nn(nt(eye_b, low).astype(BF), ones_at(iota(shape, 1) == spot + 96))
    wl[...] = table.astype(BF)

    for group in GROUPS:
        for p in group:
            turned[p] = nn(wv[...], stacked_of(p))
            if p not in GROUPS[0]:
                xs[p] = nn(wp[...], stacked_of(p))
    for group in GROUPS:
        for p, total in star_block(turned, group):
            integ[p] = dofs[p * BASIS:(p + 1) * BASIS, :] + 0.25 * total

    def flux_block(j, side, first, read):
        totals = [None] * 3
        for q in range(QUANT):
            value = read(q)
            for i in range(3):
                r = ((j * 2 + side) * QUANT + first + i) * QUANT + q
                term = flux[r:r + 1, :] * value
                totals[i] = term if totals[i] is None else totals[i] + term
        return totals

    loads[2].wait()
    for j in range(4):
        for first in range(0, QUANT, 3):
            for i, total in enumerate(flux_block(j, 0, first, lambda q: xs[q, 32 * j:32 * j + 24, :])):
                comb[first + i, 24 * j:24 * j + 24, :] = total

    unpack(rest_copies, grecv, REST_PAIRS)
    for j in range(4):
        neighbours(j, HEAD, ALL)
        nvals[j, 6] = nvals[j, 3] - nvals[j, DIFF]
    for j in range(4):
        for first in range(0, QUANT, 3):
            for i, total in enumerate(flux_block(j, 1, first, lambda q: nvals[j, q])):
                spot = (first + i, slice(24 * j, 24 * j + 24))
                comb[spot[0], spot[1], :] = comb[spot[0], spot[1], :] + total

    pushed = nt(jnp.concatenate([slip_high[0:32], slip_low[0:32]], axis=0), oht[...])
    pushed = 2.0 * (pushed[0:24] + pushed[32:56])
    for j in range(4):
        spot = slice(24 * j, 24 * j + 24)
        part = pushed[:, j * elems:(j + 1) * elems]
        comb[3, spot, :] = comb[3, spot, :] - part
        comb[6, spot, :] = comb[6, spot, :] + part

    def lifted(value):
        high, low = split(value)
        return nn(wl[...], jnp.concatenate([high, high], axis=0)) + nn(wl[:, 0:96], low)

    for p in range(QUANT):
        out[p * BASIS:(p + 1) * BASIS, :] = integ[p] + 0.25 * lifted(comb[p])

    exchange_wait(1, vsend, vrecv, v_sem, loc_sem.at[1])
    high, low = split(vrecv[...])
    both = ones_at(iota(square, 0) == part_row)
    own = nn(nt(eye_p, high).astype(BF), both) + nn(nt(eye_p, low).astype(BF), both)
    slip_out[...] = jnp.where(rank_row == 0, own[0:FACE], own[64:64 + FACE])

    for copy in head_copies + rest_copies:
        copy.wait_send()
    exchange_end(2, qsend, q_sem)
    exchange_end(1, vsend, v_sem)


def store_results(dofs_ref, slip_ref, dofs_out, slip_out, sem):
    copies = [
        pltpu.make_async_copy(source, target, sem.at[n])
        for n, (source, target) in enumerate(((dofs_ref, dofs_out), (slip_ref, slip_out)))
    ]
    for copy in copies:
        copy.start()
    for copy in copies:
        copy.wait()


def solution(mesh):
    n_row, n_col = mesh.shape["row"], mesh.shape["col"]
    devices = n_row * n_col

    def per_device(dofs, star, flux, kxi, proj, lift, orient, nbr, ocode, slist, fpart, fitem, sh0, nm0, stv, slp):
        elems = dofs.shape[1]
        vmem, anywhere = pl.BlockSpec(memory_space=pltpu.VMEM), pl.BlockSpec(memory_space=pl.ANY)
        table = pltpu.VMEM((devices, 128), F32)
        pair = pltpu.SemaphoreType.DMA((2,))
        four = pltpu.SemaphoreType.DMA((4,))
        operands = (
            dofs, star, flux, kxi, jnp.transpose(proj, (2, 0, 1)), jnp.transpose(lift, (1, 0, 2)), orient,
            nbr, ocode, slist, fpart.reshape(1, -1), fitem.reshape(1, -1), sh0, nm0, stv, slp,
        )
        inside = pl.pallas_call(
            lambda *refs: kernel(n_row, n_col, *refs),
            out_shape=(pltpu.VMEM(dofs.shape, F32), pltpu.VMEM(slp.shape, F32)),
            in_specs=[anywhere] * 16,
            out_specs=(vmem, vmem),
            scratch_shapes=[
                *(pltpu.VMEM(operand.shape, operand.dtype) for operand in operands),
                pltpu.VMEM((3 * BASIS, 192), BF),
                pltpu.VMEM((3 * BASIS, 192), BF),
                pltpu.VMEM((128, 192), BF),
                pltpu.VMEM((288, 192), F32),
                pltpu.VMEM((288, 192), BF),
                pltpu.VMEM((2, 4 * FACE, BASIS), F32),
                pltpu.VMEM((BASIS, 192), BF),
                pltpu.VMEM((2, QUANT, 3 * BASIS, elems), F32),
                pltpu.VMEM((QUANT, BASIS, elems), F32),
                pltpu.VMEM((len(BLOCKS) * 128, elems), BF),
                pltpu.VMEM((QUANT, 128, elems), F32),
                pltpu.VMEM((4, QUANT * 128, elems), BF),
                pltpu.VMEM((QUANT * 128, elems), BF),
                pltpu.VMEM((4, len(BLOCKS), 24, elems), F32),
                pltpu.VMEM((QUANT, 96, elems), F32),
                pltpu.VMEM((64, 4 * elems), F32),
                pltpu.VMEM((4 * elems, 2 * devices), BF),
                pltpu.VMEM((128, 128), F32),
                pltpu.VMEM((4, len(REST_PAIRS), BASIS, 128), F32),
                pltpu.VMEM((4, len(REST_PAIRS), BASIS, 128), F32),
                pltpu.VMEM((4, len(HEAD_PAIRS), BASIS, 128), F32),
                pltpu.VMEM((4, len(HEAD_PAIRS), BASIS, 128), F32),
                pltpu.VMEM((2 * devices, 128), F32),
                pltpu.VMEM((2 * devices, 128), F32),
                table, table,
                four, four, four, four, pair, pair, pair,
                pltpu.SemaphoreType.DMA((16,)),
            ],
            compiler_params=pltpu.CompilerParams(collective_id=0, has_side_effects=True),
        )(*operands)
        return pl.pallas_call(
            store_results,
            out_shape=(jax.ShapeDtypeStruct(dofs.shape, F32), jax.ShapeDtypeStruct(slp.shape, F32)),
            in_specs=[vmem] * 2,
            out_specs=(anywhere, anywhere),
            scratch_shapes=[pair],
            compiler_params=pltpu.CompilerParams(vmem_limit_bytes=1024 * 1024),
        )(*inside)

    split_cols = P(None, ("row", "col"))
    placed = (
        (split_cols,) * 3
        + (P(),) * 4
        + (split_cols,) * 3
        + (P(("row", "col"), None), P(("row", "col")))
        + (split_cols,) * 4
    )
    return jax.shard_map(
        per_device, mesh=mesh, in_specs=placed, out_specs=(split_cols, split_cols), check_vma=False
    )
```
